256 devices in a mesh: rep: 2 (over core), src: 16 (over z_lo, x), tgt: 8 (over z_hi, y).
Axes of the slice: x: 4, y: 4, z: 8 (z_hi: 2, z_lo: 4; z = z_hi * 4 + z_lo), core: 2. Of those that a mesh axis runs over, the one named last changes fastest.
Arguments:
- src_feats: float32 [2, 2048, 3200], P('rep', ('src', 'tgt')), may hold values from -6 to 6
- tgt_cotangent: float32 [2, 2048, 3200], P('rep', ('tgt', 'src')), may hold values from -0.6 to 0.6
- rotation: float32 [2, 16, 8, 115, 384], P('rep', 'src', 'tgt'), may hold values from -3 to 3
- edge_src: int32 [2, 16, 8, 384], P('rep', 'src', 'tgt'), may hold values from 0 to 127
- edge_tgt: int32 [2, 16, 8, 384], P('rep', 'src', 'tgt'), may hold values from 0 to 255
- edge_count: int32 [2, 16, 8], P('rep', 'src', 'tgt'), may hold values from 192 to 384, as said below
- w_zero: float32 [640, 640], replicated, may hold values from -0.25 to 0.25
- w_one_re: float32 [512, 512], replicated, may hold values from -0.1875 to 0.1875
- w_one_im: float32 [512, 512], replicated, may hold values from -0.1875 to 0.1875
- w_two_re: float32 [384, 384], replicated, may hold values from -0.21875 to 0.21875
- w_two_im: float32 [384, 384], replicated, may hold values from -0.21875 to 0.21875
Outputs:
- grad_feats: float32 [2, 2048, 3200], P('rep', ('src', 'tgt'))
- grad_w_zero: float32 [640, 640], P('src')
- grad_w_one_re: float32 [512, 512], P('src')
- grad_w_one_im: float32 [512, 512], P('src')
- grad_w_two_re: float32 [384, 384], P('src')
- grad_w_two_im: float32 [384, 384], P('src')
The draws below stay inside these ranges and needn't reach their ends.
Inputs may be any that keep to these rules, and one draw needn't show every extreme that they name: `edge_count`: some tile of each structure is full.
All inputs are finite; a program needn't handle non-finite values.
Results may differ from the reference program's by a relative error of at most 0.0003.
Values sent between devices are 32-bit elements; how exact they have to be, the bound alone decides.
A program may use at most 128 MiB of HBM per device.

```python
import jax
import jax.numpy as jnp
from jax import lax

CH = 128
ROT = 115
EDGE_CAP = 384
STRUCTS = 2
ATOMS = 2048
SRC_BLK = 128
TGT_BLK = 256
FEAT = 3200
N_SRC = 16
N_TGT = 8


def draw_edge_src(key, part):
    return jax.random.randint(jax.random.fold_in(key, 11), (STRUCTS, N_SRC, N_TGT, EDGE_CAP), 0, SRC_BLK, dtype=jnp.int32)


def draw_edge_tgt(key, part):
    return jax.random.randint(jax.random.fold_in(key, 23), (STRUCTS, N_SRC, N_TGT, EDGE_CAP), 0, TGT_BLK, dtype=jnp.int32)


def draw_edge_count(key, part):
    first, third = jax.random.split(jax.random.fold_in(key, 37), 2)
    tiles = N_SRC * N_TGT
    base = jax.random.randint(first, (STRUCTS, tiles), EDGE_CAP // 2, EDGE_CAP + 1, dtype=jnp.int32)
    picked = jax.random.randint(third, (STRUCTS, 1), 0, tiles, dtype=jnp.int32)
    full = jnp.arange(tiles, dtype=jnp.int32)[None, :] == picked
    counts = jnp.where(full, EDGE_CAP, base).astype(jnp.int32)
    return counts.reshape(STRUCTS, N_SRC, N_TGT)


def block_scale(stream_key, dims, cuts, least, top_value):
    gain, own = 1.0, jax.random.fold_in(stream_key, 6)
    for dim, blocks in cuts:
        heights = jnp.exp(jax.random.uniform(jax.random.fold_in(own, dim), (blocks,), jnp.float32, least / len(cuts), top_value / len(cuts)))
        gain = gain * jnp.repeat(heights, dims[dim] // blocks).reshape([-1 if axis == dim else 1 for axis in range(len(dims))])
    return gain


def gaussian(stream_key, dims, spread, limit, shards=(), kind=jnp.bfloat16):
    array = jax.random.normal(stream_key, dims, jnp.float32) * spread
    if len(shards) > 0:
        array = block_scale(stream_key, dims, shards, -0.22, 0.18) * array
    return jnp.clip(array, min=-limit, max=limit).astype(kind)


def setup_inputs(seed: int = 0) -> dict:
    splits = jax.random.split(jax.random.key(seed), 12)
    return {
        "src_feats": gaussian(splits[0], (STRUCTS, ATOMS, FEAT), 1.0, 6.0, ((0, 2), (1, 128)), jnp.float32),
        "tgt_cotangent": gaussian(splits[1], (STRUCTS, ATOMS, FEAT), 0.1, 0.6, ((0, 2), (1, 128)), jnp.float32),
        "rotation": gaussian(splits[2], (STRUCTS, N_SRC, N_TGT, ROT, EDGE_CAP), 0.45, 3.0, ((0, 2), (1, 16), (2, 8)), jnp.float32),
        "edge_src": draw_edge_src(jax.random.fold_in(splits[11], 71), 0),
        "edge_tgt": draw_edge_tgt(jax.random.fold_in(splits[11], 71), 0),
        "edge_count": draw_edge_count(jax.random.fold_in(splits[11], 71), 0),
        "w_zero": gaussian(splits[6], (5 * CH, 5 * CH), (5 * CH) ** -0.5, 0.25, (), jnp.float32),
        "w_one_re": gaussian(splits[7], (4 * CH, 4 * CH), (8 * CH) ** -0.5, 0.1875, (), jnp.float32),
        "w_one_im": gaussian(splits[8], (4 * CH, 4 * CH), (8 * CH) ** -0.5, 0.1875, (), jnp.float32),
        "w_two_re": gaussian(splits[9], (3 * CH, 3 * CH), (6 * CH) ** -0.5, 0.21875, (), jnp.float32),
        "w_two_im": gaussian(splits[10], (3 * CH, 3 * CH), (6 * CH) ** -0.5, 0.21875, (), jnp.float32),
    }


OFFSETS = (0, 1, 10, 35, 70)
HIGH = lax.Precision.HIGHEST


def rotations(wig):
    mats = []
    for level in range(5):
        order = min(level, 2)
        rows = 2 * order + 1
        cols = 2 * level + 1
        piece = wig[OFFSETS[level]:OFFSETS[level] + rows * cols]
        mats.append(piece.reshape(rows, cols, piece.shape[-1]))
    return mats


def group(rotated, count):
    zero = jnp.stack([rotated[v][:, min(v, 2)] for v in range(5)], 1)
    plus_one = jnp.stack([rotated[v][:, min(v, 2) + 1] for v in range(1, 5)], 1)
    minus_one = jnp.stack([rotated[v][:, min(v, 2) - 1] for v in range(1, 5)], 1)
    plus_two = jnp.stack([rotated[v][:, 4] for v in range(2, 5)], 1)
    minus_two = jnp.stack([rotated[v][:, 0] for v in range(2, 5)], 1)
    return tuple(a.reshape(count, -1) for a in (zero, plus_one, minus_one, plus_two, minus_two))


def ungroup(groups, count, chans):
    zero, plus_one, minus_one, plus_two, minus_two = [a.reshape(count, -1, chans) for a in groups]
    result = []
    for level in range(5):
        rows = []
        if level >= 2:
            rows.append(minus_two[:, level - 2])
        if level >= 1:
            rows.append(minus_one[:, level - 1])
        rows.append(zero[:, level])
        if level >= 1:
            rows.append(plus_one[:, level - 1])
        if level >= 2:
            rows.append(plus_two[:, level - 2])
        result.append(jnp.stack(rows, 1))
    return result


def tdot(left, right):
    return lax.dot_general(left, right, (((0,), (0,)), ((), ())), precision=HIGH, preferred_element_type=jnp.float32)


def ntdot(left, right):
    return lax.dot_general(left, right, (((1,), (1,)), ((), ())), precision=HIGH, preferred_element_type=jnp.float32)


def block_grads(xrows, grows, wig, weights):
    w_zero, w_one_re, w_one_im, w_two_re, w_two_im = weights
    count, coefs, chans = xrows.shape
    mats = rotations(wig)
    xrot = [jnp.einsum('rcb,bcf->brf', mats[v], xrows[:, v * v:(v + 1) * (v + 1)], precision=HIGH) for v in range(5)]
    grot = [jnp.einsum('rcb,bcf->brf', mats[v], grows[:, v * v:(v + 1) * (v + 1)], precision=HIGH) for v in range(5)]
    z0, zp1, zm1, zp2, zm2 = group(xrot, count)
    u0, up1, um1, up2, um2 = group(grot, count)
    grads = (tdot(z0, u0), tdot(zp1, up1) + tdot(zm1, um1), tdot(zp1, um1) - tdot(zm1, up1),
             tdot(zp2, up2) + tdot(zm2, um2), tdot(zp2, um2) - tdot(zm2, up2))
    d0 = ntdot(u0, w_zero)
    dp1 = ntdot(up1, w_one_re) + ntdot(um1, w_one_im)
    dm1 = ntdot(um1, w_one_re) - ntdot(up1, w_one_im)
    dp2 = ntdot(up2, w_two_re) + ntdot(um2, w_two_im)
    dm2 = ntdot(um2, w_two_re) - ntdot(up2, w_two_im)
    back = ungroup((d0, dp1, dm1, dp2, dm2), count, chans)
    pieces = [jnp.einsum('rcb,brf->bcf', mats[v], back[v], precision=HIGH) for v in range(5)]
    return jnp.concatenate(pieces, 1), grads


def reference(src_feats, tgt_cotangent, rotation, edge_src, edge_tgt, edge_count, w_zero, w_one_re, w_one_im, w_two_re, w_two_im):
    weights = (w_zero, w_one_re, w_one_im, w_two_re, w_two_im)
    structs, atoms, feat = src_feats.shape
    chans = w_zero.shape[0] // 5
    nsrc, ntgt, cap = edge_src.shape[1], edge_src.shape[2], edge_src.shape[3]
    src_blk = atoms // nsrc
    tgt_blk = atoms // ntgt
    grads = tuple(jnp.zeros(w.shape, jnp.float32) for w in weights)
    outputs = []
    for which in range(structs):
        xall = src_feats[which].reshape(atoms, 25, chans)
        gall = tgt_cotangent[which].reshape(atoms, 25, chans)

        def tile(carry, index):
            total, sums = carry
            row = index // ntgt
            col = index % ntgt
            sources = (edge_src[which][row, col] + row * src_blk).astype(jnp.int32)
            targets = (edge_tgt[which][row, col] + col * tgt_blk).astype(jnp.int32)
            live = (jnp.arange(cap, dtype=jnp.int32) < edge_count[which][row, col]).astype(jnp.float32)
            xrows = xall[sources] * live[:, None, None]
            grows = gall[targets] * live[:, None, None]
            term, parts = block_grads(xrows, grows, rotation[which][row, col], weights)
            total = total.at[sources].add(term)
            return (total, tuple(a + b for a, b in zip(sums, parts))), None

        init = (jnp.zeros((atoms, 25, chans), jnp.float32), grads)
        (total, grads), unused = lax.scan(tile, init, jnp.arange(nsrc * ntgt, dtype=jnp.int32))
        outputs.append(total.reshape(atoms, feat))
    grad_feats = jnp.stack(outputs, 0)
    return (grad_feats, grads[0], grads[1], grads[2], grads[3], grads[4])
```

```python
import jax
import jax.numpy as jnp
from jax import lax
from jax.experimental import pallas as pl
from jax.experimental.pallas import tpu as pltpu
from jax.sharding import PartitionSpec as P

OFFSETS = (0, 1, 10, 35, 70)
F32, BF16 = jnp.float32, jnp.bfloat16
NT = (((1,), (1,)), ((), ()))
NN = (((1,), (0,)), ((), ()))


def mm(a, b, dims):
    return lax.dot_general(a, b, dims, preferred_element_type=F32)


def split(a):
    hi = a.astype(BF16)
    return hi, (a - hi.astype(F32)).astype(BF16)


def onehot(ids, live, atoms):
    rows = lax.broadcasted_iota(jnp.int32, (atoms, ids.shape[1]), 0)
    return jnp.where((rows == ids) & live, 1.0, 0.0).astype(BF16)


def pick(block_ref, hot_ref, out_ref, chans):
    def one(c, carry):
        at = pl.multiple_of(c * chans, chans)
        hi, lo = split(block_ref[:, pl.ds(at, chans)].T)
        out_ref[pl.ds(at, chans), :] = mm(jnp.concatenate([hi, lo], 1), hot_ref[...], NN)
        return carry

    lax.fori_loop(0, out_ref.shape[0] // chans, one, 0)


def rotate(rows_ref, rot_ref, put, chans, cap):
    steps, lanes = 16, 128
    tiles = cap // lanes

    def one(i, carry):
        ch = pl.multiple_of((i // tiles) * steps, steps)
        ln = pl.multiple_of((i % tiles) * lanes, lanes)
        for level in range(5):
            q, cols = min(level, 2), 2 * level + 1
            xs = [
                rows_ref[pl.ds((level * level + c) * chans + ch, steps), pl.ds(ln, lanes)]
                for c in range(cols)
            ]
            for r in range(2 * q + 1):
                acc = None
                for c in range(cols):
                    o = OFFSETS[level] + r * cols + c
                    term = rot_ref[o : o + 1, pl.ds(ln, lanes)] * xs[c]
                    acc = term if acc is None else acc + term
                m = r - q
                put(abs(m), m < 0, level - abs(m), ch, ln, acc)
        return carry

    lax.fori_loop(0, (chans // steps) * tiles, one, 0)


def compute_kernel(
    cnt_ref, x_ref, g_ref, rot_ref, es_ref, et_ref,
    w0_ref, w1r_ref, w1i_ref, w2r_ref, w2i_ref,
    total_ref, wg_ref,
    hs_ref, ht_ref, hs2_ref, rows_ref,
    z0_ref, z1_ref, z2_ref, u0_ref, u1_ref, u2_ref, v1_ref, v2_ref,
    wh0, wh1r, wh1i, wh2r, wh2i, d0_ref, d1_ref, d2_ref, term_ref,
):
    cap = es_ref.shape[1]
    chans = w0_ref.shape[0] // 5
    src_blk, tgt_blk = x_ref.shape[0], g_ref.shape[0]
    live = lax.broadcasted_iota(jnp.int32, (1, cap), 1) < cnt_ref[0]
    hot = onehot(es_ref[...], live, src_blk)
    hs_ref[:src_blk, :] = hot
    hs_ref[src_blk:, :] = hot
    hs2_ref[:, :cap] = hot
    hs2_ref[:, cap:] = hot
    hot = onehot(et_ref[...], live, tgt_blk)
    ht_ref[:tgt_blk, :] = hot
    ht_ref[tgt_blk:, :] = hot

    zrefs = (z0_ref, z1_ref, z2_ref)

    def put_z(order, neg, k, ch, ln, val):
        hi, lo = split(val)
        rows = pl.ds(k * chans + ch, 16)
        at = pl.ds(ln + (cap if neg else 0), 128)
        zrefs[order][0, rows, at] = hi
        zrefs[order][1, rows, at] = lo

    pick(x_ref, hs_ref, rows_ref, chans)
    rotate(rows_ref, rot_ref, put_z, chans, cap)

    urefs = (u0_ref, u1_ref, u2_ref)
    vrefs = (None, v1_ref, v2_ref)

    def put_u(order, neg, k, ch, ln, val):
        hi, lo = split(val)
        rows = pl.ds(k * chans + ch, 16)
        at = pl.ds(ln + (cap if neg else 0), 128)
        urefs[order][0, rows, at] = hi
        urefs[order][1, rows, at] = lo
        if order:
            at = pl.ds(ln + (0 if neg else cap), 128)
            vrefs[order][0, rows, at] = hi if neg else -hi
            vrefs[order][1, rows, at] = lo if neg else -lo

    pick(g_ref, ht_ref, rows_ref, chans)
    rotate(rows_ref, rot_ref, put_u, chans, cap)

    def grad(z, u, at, count):
        zh, zl = z[0, pl.ds(at, count), :], z[1, pl.ds(at, count), :]
        return mm(zh, u[0], NT) + mm(zh, u[1], NT) + mm(zl, u[0], NT)

    owners = wg_ref.shape[0]
    half = owners // 2

    def grads(h, carry):
        base = 0
        for z, u, cols in (
            (z0_ref, u0_ref, 5), (z1_ref, u1_ref, 4), (z1_ref, v1_ref, 4), (z2_ref, u2_ref, 3), (z2_ref, v2_ref, 3),
        ):
            per = cols * chans // owners
            res = grad(z, u, pl.multiple_of(h * half * per, 16), half * per)
            for s in range(half):
                for j in range(cols):
                    wg_ref[h * half + s, base + j * per : base + (j + 1) * per, :] = res[
                        s * per : (s + 1) * per, j * chans : (j + 1) * chans
                    ]
            base += cols * per
        return carry

    lax.fori_loop(0, 2, grads, 0)

    for src, dst in ((w0_ref, wh0), (w1r_ref, wh1r), (w1i_ref, wh1i), (w2r_ref, wh2r), (w2i_ref, wh2i)):
        def cut(i, carry, src=src, dst=dst):
            at = pl.ds(pl.multiple_of(i * 128, 128), 128)
            dst[0, at, :], dst[1, at, :] = split(src[at, :])
            return carry

        lax.fori_loop(0, src.shape[0] // 128, cut, 0)

    def three(w, u, at):
        wh, wl = w[0, at, :], w[1, at, :]
        return mm(wh, u[0], NN) + mm(wh, u[1], NN) + mm(wl, u[0], NN)

    for at in (pl.ds(0, 320), pl.ds(320, 320)):
        d0_ref[at, :] = three(wh0, u0_ref, at)
    for at in (pl.ds(0, 256), pl.ds(256, 256)):
        d1_ref[at, :] = three(wh1r, u1_ref, at) + three(wh1i, v1_ref, at)
    for at in (pl.ds(0, 192), pl.ds(192, 192)):
        d2_ref[at, :] = three(wh2r, u2_ref, at) + three(wh2i, v2_ref, at)

    drefs = (d0_ref, d1_ref, d2_ref)
    tiles = cap // 128

    def back(i, carry):
        ch = pl.multiple_of((i // tiles) * 16, 16)
        ln = pl.multiple_of((i % tiles) * 128, 128)
        for level in range(5):
            q, cols = min(level, 2), 2 * level + 1
            ds = []
            for r in range(2 * q + 1):
                m = r - q
                k = level - abs(m)
                ds.append(drefs[abs(m)][pl.ds(k * chans + ch, 16), pl.ds(ln + (cap if m < 0 else 0), 128)])
            for c in range(cols):
                acc = None
                for r in range(2 * q + 1):
                    o = OFFSETS[level] + r * cols + c
                    term = rot_ref[o : o + 1, pl.ds(ln, 128)] * ds[r]
                    acc = term if acc is None else acc + term
                hi, lo = split(acc)
                rows = pl.ds((level * level + c) * chans + ch, 16)
                term_ref[rows, pl.ds(ln, 128)] = hi
                term_ref[rows, pl.ds(ln + cap, 128)] = lo
        return carry

    lax.fori_loop(0, (chans // 16) * tiles, back, 0)

    def scatter(c, carry):
        at = pl.multiple_of(c * 5 * chans, chans)
        total_ref[:, pl.ds(at, 5 * chans)] = mm(hs2_ref[...], term_ref[pl.ds(at, 5 * chans), :], NT)
        return carry

    lax.fori_loop(0, 5, scatter, 0)


def compute(xb, gb, wig, es, et, cnt, weights, owners):
    cap = es.shape[1]
    chans = weights[0].shape[0] // 5
    src_blk, feat = xb.shape
    tgt_blk = gb.shape[0]
    per = 600
    vm = pl.BlockSpec(memory_space=pltpu.VMEM)
    dims = [w.shape[0] for w in weights]
    scratch = [
        pltpu.VMEM((2 * src_blk, cap), BF16),
        pltpu.VMEM((2 * tgt_blk, cap), BF16),
        pltpu.VMEM((src_blk, 2 * cap), BF16),
        pltpu.VMEM((feat, cap), F32),
        pltpu.VMEM((2, dims[0], cap), BF16),
        pltpu.VMEM((2, dims[1], 2 * cap), BF16),
        pltpu.VMEM((2, dims[3], 2 * cap), BF16),
        pltpu.VMEM((2, dims[0], cap), BF16),
        pltpu.VMEM((2, dims[1], 2 * cap), BF16),
        pltpu.VMEM((2, dims[3], 2 * cap), BF16),
        pltpu.VMEM((2, dims[1], 2 * cap), BF16),
        pltpu.VMEM((2, dims[3], 2 * cap), BF16),
        *[pltpu.VMEM((2, d, d), BF16) for d in dims],
        pltpu.VMEM((dims[0], cap), F32),
        pltpu.VMEM((dims[1], 2 * cap), F32),
        pltpu.VMEM((dims[3], 2 * cap), F32),
        pltpu.VMEM((feat, 2 * cap), BF16),
    ]
    return pl.pallas_call(
        compute_kernel,
        out_shape=(
            jax.ShapeDtypeStruct((src_blk, feat), F32),
            jax.ShapeDtypeStruct((owners, per, chans), F32),
        ),
        in_specs=[pl.BlockSpec(memory_space=pltpu.SMEM)] + [vm] * 10,
        out_specs=(vm, vm),
        scratch_shapes=scratch,
        compiler_params=pltpu.CompilerParams(vmem_limit_bytes=60 * 2**20),
        name="tile",
    )(cnt, xb, gb, wig, es, et, *weights)


def unpack(packed, weights, owners, chans):
    outs, base = [], 0
    for w in weights:
        cols = w.shape[0] // chans
        per = w.shape[0] // owners
        piece = packed[base : base + cols * per].reshape(cols, per, chans)
        outs.append(piece.transpose(1, 0, 2).reshape(per, cols * chans))
        base += cols * per
    return outs


def local(src_feats, tgt_cotangent, rotation, edge_src, edge_tgt, edge_count, *weights):
    chans = weights[0].shape[0] // 5
    owners = lax.axis_size("src")
    xb = lax.all_gather(src_feats[0], "tgt", axis=0, tiled=True)
    gb = lax.all_gather(tgt_cotangent[0], "src", axis=0, tiled=True)
    total, wg = compute(
        xb, gb, rotation[0, 0, 0], edge_src[0, 0], edge_tgt[0, 0], edge_count[0, 0], weights, owners
    )
    part = lax.psum_scatter(wg, "src", scatter_dimension=0, tiled=True)[0]
    grad_feats = lax.psum_scatter(total[None], "tgt", scatter_dimension=1, tiled=True)
    packed = lax.psum(part, ("rep", "tgt"))
    return (grad_feats, *unpack(packed, weights, owners, chans))


def solution(mesh):
    placed = (
        P("rep", ("src", "tgt"), None),
        P("rep", ("tgt", "src"), None),
        P("rep", "src", "tgt", None, None),
        P("rep", "src", "tgt", None),
        P("rep", "src", "tgt", None),
        P("rep", "src", "tgt"),
        P(), P(), P(), P(), P(),
    )
    return jax.shard_map(
        local,
        mesh=mesh,
        in_specs=placed,
        out_specs=(P("rep", ("src", "tgt"), None), *[P("src", None)] * 5),
        check_vma=False,
    )
```

```python
import jax
import jax.numpy as jnp
from jax import lax
from jax.experimental import pallas as pl
from jax.experimental.pallas import tpu as pltpu
from jax.sharding import PartitionSpec as P

OFFSETS = (0, 1, 10, 35, 70)
F32, BF16 = jnp.float32, jnp.bfloat16
MESH = pl.DeviceIdType.MESH
PACK = 640
NT = (((1,), (1,)), ((), ()))
NN = (((1,), (0,)), ((), ()))


def mm(a, b, dims):
    return lax.dot_general(a, b, dims, preferred_element_type=F32)


def split(a):
    hi = a.astype(BF16)
    return hi, (a - hi.astype(F32)).astype(BF16)


def onehot(ids, live, atoms):
    rows = lax.broadcasted_iota(jnp.int32, (atoms, ids.shape[1]), 0)
    return jnp.where((rows == ids) & live, 1.0, 0.0).astype(BF16)


def pick(block_ref, hot_ref, out_ref, chans):
    def one(c, carry):
        at = pl.multiple_of(c * chans, chans)
        hi, lo = split(block_ref[:, pl.ds(at, chans)].T)
        out_ref[pl.ds(at, chans), :] = mm(jnp.concatenate([hi, lo], 1), hot_ref[...], NN)
        return carry

    lax.fori_loop(0, out_ref.shape[0] // chans, one, 0)


def rotate(rows_ref, rot_ref, put, chans, cap):
    steps, lanes = 16, 128
    tiles = cap // lanes

    def one(i, carry):
        ch = pl.multiple_of((i // tiles) * steps, steps)
        ln = pl.multiple_of((i % tiles) * lanes, lanes)
        for level in range(5):
            q, cols = min(level, 2), 2 * level + 1
            xs = [
                rows_ref[pl.ds((level * level + c) * chans + ch, steps), pl.ds(ln, lanes)]
                for c in range(cols)
            ]
            for r in range(2 * q + 1):
                acc = None
                for c in range(cols):
                    o = OFFSETS[level] + r * cols + c
                    term = rot_ref[o : o + 1, pl.ds(ln, lanes)] * xs[c]
                    acc = term if acc is None else acc + term
                m = r - q
                put(abs(m), m < 0, level - abs(m), ch, ln, acc)
        return carry

    lax.fori_loop(0, (chans // steps) * tiles, one, 0)


def compute_kernel(
    cnt_ref, x_ref, g_ref, rot_ref, es_ref, et_ref,
    w0_ref, w1r_ref, w1i_ref, w2r_ref, w2i_ref,
    total_ref, wg_ref,
    hs_ref, ht_ref, hs2_ref, rows_ref,
    z0_ref, z1_ref, z2_ref, u0_ref, u1_ref, u2_ref, v1_ref, v2_ref,
    wh0, wh1r, wh1i, wh2r, wh2i, d0_ref, d1_ref, d2_ref, term_ref,
):
    cap = es_ref.shape[1]
    chans = w0_ref.shape[0] // 5
    src_blk, tgt_blk = x_ref.shape[0], g_ref.shape[0]
    live = lax.broadcasted_iota(jnp.int32, (1, cap), 1) < cnt_ref[0]
    hot = onehot(es_ref[...], live, src_blk)
    hs_ref[:src_blk, :] = hot
    hs_ref[src_blk:, :] = hot
    hs2_ref[:, :cap] = hot
    hs2_ref[:, cap:] = hot
    hot = onehot(et_ref[...], live, tgt_blk)
    ht_ref[:tgt_blk, :] = hot
    ht_ref[tgt_blk:, :] = hot

    zrefs = (z0_ref, z1_ref, z2_ref)

    def put_z(order, neg, k, ch, ln, val):
        hi, lo = split(val)
        rows = pl.ds(k * chans + ch, 16)
        at = pl.ds(ln + (cap if neg else 0), 128)
        zrefs[order][0, rows, at] = hi
        zrefs[order][1, rows, at] = lo

    pick(x_ref, hs_ref, rows_ref, chans)
    rotate(rows_ref, rot_ref, put_z, chans, cap)

    urefs = (u0_ref, u1_ref, u2_ref)
    vrefs = (None, v1_ref, v2_ref)

    def put_u(order, neg, k, ch, ln, val):
        hi, lo = split(val)
        rows = pl.ds(k * chans + ch, 16)
        at = pl.ds(ln + (cap if neg else 0), 128)
        urefs[order][0, rows, at] = hi
        urefs[order][1, rows, at] = lo
        if order:
            at = pl.ds(ln + (0 if neg else cap), 128)
            vrefs[order][0, rows, at] = hi if neg else -hi
            vrefs[order][1, rows, at] = lo if neg else -lo

    pick(g_ref, ht_ref, rows_ref, chans)
    rotate(rows_ref, rot_ref, put_u, chans, cap)

    def grad(z, u, at, count):
        zh, zl = z[0, pl.ds(at, count), :], z[1, pl.ds(at, count), :]
        return mm(zh, u[0], NT) + mm(zh, u[1], NT) + mm(zl, u[0], NT)

    owners = wg_ref.shape[0]
    half = owners // 2

    def grads(h, carry):
        base = 0
        for z, u, cols in (
            (z0_ref, u0_ref, 5), (z1_ref, u1_ref, 4), (z1_ref, v1_ref, 4), (z2_ref, u2_ref, 3), (z2_ref, v2_ref, 3),
        ):
            per = cols * chans // owners
            res = grad(z, u, pl.multiple_of(h * half * per, 16), half * per)
            for s in range(half):
                for j in range(cols):
                    wg_ref[h * half + s, base + j * per : base + (j + 1) * per, :] = res[
                        s * per : (s + 1) * per, j * chans : (j + 1) * chans
                    ]
            base += cols * per
        wg_ref[pl.ds(h * half, half), base:, :] = jnp.zeros((half, wg_ref.shape[1] - base, chans), F32)
        return carry

    lax.fori_loop(0, 2, grads, 0)

    for src, dst in ((w0_ref, wh0), (w1r_ref, wh1r), (w1i_ref, wh1i), (w2r_ref, wh2r), (w2i_ref, wh2i)):
        def cut(i, carry, src=src, dst=dst):
            at = pl.ds(pl.multiple_of(i * 128, 128), 128)
            dst[0, at, :], dst[1, at, :] = split(src[at, :])
            return carry

        lax.fori_loop(0, src.shape[0] // 128, cut, 0)

    def three(w, u, at):
        wh, wl = w[0, at, :], w[1, at, :]
        return mm(wh, u[0], NN) + mm(wh, u[1], NN) + mm(wl, u[0], NN)

    for at in (pl.ds(0, 320), pl.ds(320, 320)):
        d0_ref[at, :] = three(wh0, u0_ref, at)
    for at in (pl.ds(0, 256), pl.ds(256, 256)):
        d1_ref[at, :] = three(wh1r, u1_ref, at) + three(wh1i, v1_ref, at)
    for at in (pl.ds(0, 192), pl.ds(192, 192)):
        d2_ref[at, :] = three(wh2r, u2_ref, at) + three(wh2i, v2_ref, at)

    drefs = (d0_ref, d1_ref, d2_ref)
    tiles = cap // 128

    def back(i, carry):
        ch = pl.multiple_of((i // tiles) * 16, 16)
        ln = pl.multiple_of((i % tiles) * 128, 128)
        for level in range(5):
            q, cols = min(level, 2), 2 * level + 1
            ds = []
            for r in range(2 * q + 1):
                m = r - q
                k = level - abs(m)
                ds.append(drefs[abs(m)][pl.ds(k * chans + ch, 16), pl.ds(ln + (cap if m < 0 else 0), 128)])
            for c in range(cols):
                acc = None
                for r in range(2 * q + 1):
                    o = OFFSETS[level] + r * cols + c
                    term = rot_ref[o : o + 1, pl.ds(ln, 128)] * ds[r]
                    acc = term if acc is None else acc + term
                hi, lo = split(acc)
                rows = pl.ds((level * level + c) * chans + ch, 16)
                term_ref[rows, pl.ds(ln, 128)] = hi
                term_ref[rows, pl.ds(ln + cap, 128)] = lo
        return carry

    lax.fori_loop(0, (chans // 16) * tiles, back, 0)

    def scatter(c, carry):
        at = pl.multiple_of(c * 5 * chans, chans)
        total_ref[:, pl.ds(at, 5 * chans)] = mm(hs2_ref[...], term_ref[pl.ds(at, 5 * chans), :], NT)
        return carry

    lax.fori_loop(0, 5, scatter, 0)


def compute(xb, gb, wig, es, et, cnt, weights, owners):
    cap = es.shape[1]
    chans = weights[0].shape[0] // 5
    src_blk, feat = xb.shape
    tgt_blk = gb.shape[0]
    per = PACK
    vm = pl.BlockSpec(memory_space=pltpu.VMEM)
    dims = [w.shape[0] for w in weights]
    scratch = [
        pltpu.VMEM((2 * src_blk, cap), BF16),
        pltpu.VMEM((2 * tgt_blk, cap), BF16),
        pltpu.VMEM((src_blk, 2 * cap), BF16),
        pltpu.VMEM((feat, cap), F32),
        pltpu.VMEM((2, dims[0], cap), BF16),
        pltpu.VMEM((2, dims[1], 2 * cap), BF16),
        pltpu.VMEM((2, dims[3], 2 * cap), BF16),
        pltpu.VMEM((2, dims[0], cap), BF16),
        pltpu.VMEM((2, dims[1], 2 * cap), BF16),
        pltpu.VMEM((2, dims[3], 2 * cap), BF16),
        pltpu.VMEM((2, dims[1], 2 * cap), BF16),
        pltpu.VMEM((2, dims[3], 2 * cap), BF16),
        *[pltpu.VMEM((2, d, d), BF16) for d in dims],
        pltpu.VMEM((dims[0], cap), F32),
        pltpu.VMEM((dims[1], 2 * cap), F32),
        pltpu.VMEM((dims[3], 2 * cap), F32),
        pltpu.VMEM((feat, 2 * cap), BF16),
    ]
    return pl.pallas_call(
        compute_kernel,
        out_shape=(
            jax.ShapeDtypeStruct((src_blk, feat), F32),
            jax.ShapeDtypeStruct((owners, per, chans), F32),
        ),
        in_specs=[pl.BlockSpec(memory_space=pltpu.SMEM)] + [vm] * 10,
        out_specs=(vm, vm),
        scratch_shapes=scratch,
        compiler_params=pltpu.CompilerParams(vmem_limit_bytes=60 * 2**20),
        name="tile",
    )(cnt, xb, gb, wig, es, et, *weights)


def place():
    rep, src, tgt = lax.axis_index("rep"), lax.axis_index("src"), lax.axis_index("tgt")
    return rep, src // 4, src % 4, tgt // 4, tgt % 4


def device(rep, zl, x, zh, y):
    return (rep, zl * 4 + x, zh * 4 + y)


def pair(i, d):
    return (i + 1 - 2 * (i % 2), (i + 2) % 4, 3 - i)[d - 1]


class Copies:
    def __init__(self, send, recv):
        self.send, self.recv, self.made = send, recv, []

    def start(self, src, dst, to):
        n = len(self.made)
        copy = pltpu.make_async_remote_copy(
            src_ref=src, dst_ref=dst, send_sem=self.send.at[n], recv_sem=self.recv.at[n],
            device_id=to, device_id_type=MESH,
        )
        copy.start()
        self.made.append(copy)
        return copy

    def drain(self):
        for copy in self.made:
            copy.wait_send()


def greet(peers):
    barrier = pltpu.get_barrier_semaphore()
    for peer in peers:
        pl.semaphore_signal(barrier, inc=1, device_id=peer, device_id_type=MESH)
    pl.semaphore_wait(barrier, len(peers))


def gather_kernel(x_in, g_in, x_out, g_out, send, recv, own):
    rep, zl, x, zh, y = place()
    right, left = (x + 1) % 4, (x + 3) % 4
    up, down = (y + 1) % 4, (y + 3) % 4
    lines = [pair(zl, d) for d in (1, 2, 3)]

    def on_x(nx):
        return device(rep, zl, nx, zh, y)

    def on_y(ny):
        return device(rep, zl, x, zh, ny)

    def on_z(nz):
        return device(rep, nz, x, zh, y)

    across = device(rep, zl, x, 1 - zh, y)
    greet([*[on_z(p) for p in lines], on_x(left), on_x(right), on_y(down), on_y(up), across])
    far = Copies(send, recv)
    mine_g, mine_x = zl * 4 + x, zh * 4 + y
    zs = [far.start(g_in, g_out.at[mine_g], on_z(p)) for p in lines]
    hop = far.start(x_in, x_out.at[mine_x], across)

    def both(ref, slot, out, to, one, other):
        return (
            far.start(ref, out.at[slot], to(one)),
            far.start(ref, out.at[slot], to(other)),
        )

    def relay(copies, out, slots, to, one, other):
        copies[0].wait_recv()
        a = far.start(out.at[slots[0], :8], out.at[slots[0], :8], to(one))
        copies[1].wait_recv()
        b = far.start(out.at[slots[1], 8:], out.at[slots[1], 8:], to(other))
        return a, b

    xs = [both(g_in, mine_g, g_out, on_x, right, left)]
    ys = [both(x_in, mine_x, x_out, on_y, up, down)]
    keep = [
        pltpu.make_async_copy(g_in, g_out.at[mine_g], own.at[0]),
        pltpu.make_async_copy(x_in, x_out.at[mine_x], own.at[1]),
    ]
    for copy in keep:
        copy.start()
    ends = []
    order = [zl, *lines]

    def x_step(j):
        zs[j - 1].wait_recv()
        slot = order[j] * 4 + x
        xs.append(both(g_out.at[slot], slot, g_out, on_x, right, left))

    def x_relay(j):
        ends.extend(relay(xs[j], g_out, (order[j] * 4 + left, order[j] * 4 + right), on_x, right, left))

    def y_relay(j):
        at = (zh, 1 - zh)[j] * 4
        ends.extend(relay(ys[j], x_out, (at + down, at + up), on_y, up, down))

    x_step(1)
    x_relay(0)
    y_relay(0)
    x_step(2)
    x_relay(1)
    hop.wait_recv()
    slot = (1 - zh) * 4 + y
    ys.append(both(x_out.at[slot], slot, x_out, on_y, up, down))
    x_step(3)
    x_relay(2)
    y_relay(1)
    x_relay(3)
    for copy in ends:
        copy.wait_recv()
    for copy in keep:
        copy.wait()
    far.drain()


def gather(src_feats, tgt_cotangent, n_src, n_tgt):
    rows, feat = src_feats.shape
    vm = pl.BlockSpec(memory_space=pltpu.VMEM)
    count = 28
    return pl.pallas_call(
        gather_kernel,
        out_shape=(
            jax.ShapeDtypeStruct((n_tgt, rows, feat), F32),
            jax.ShapeDtypeStruct((n_src, rows, feat), F32),
        ),
        in_specs=[vm, vm],
        out_specs=(vm, vm),
        scratch_shapes=[
            pltpu.SemaphoreType.DMA((count,)),
            pltpu.SemaphoreType.DMA((count,)),
            pltpu.SemaphoreType.DMA((2,)),
        ],
        compiler_params=pltpu.CompilerParams(
            collective_id=0, has_side_effects=True, vmem_limit_bytes=40 * 2**20
        ),
        name="spread",
    )(src_feats, tgt_cotangent)


def ring_first(far, me, part, hops, to):
    right, left, opp = (me + 1) % 4, (me + 3) % 4, (me + 2) % 4
    return (
        far.start(part(opp, 0), hops.at[0], to(right)),
        far.start(part(opp, 1), hops.at[1], to(left)),
    )


def ring_rest(far, me, part, firsts, hops, ins, to):
    right, left = (me + 1) % 4, (me + 3) % 4
    made = [
        far.start(part(right, 1), ins.at[0, 1], to(right)),
        far.start(part(left, 0), ins.at[1, 0], to(left)),
    ]
    firsts[0].wait_recv()
    hops[0] = hops[0] + part(right, 0)[...]
    made.append(far.start(hops.at[0], ins.at[0, 0], to(right)))
    firsts[1].wait_recv()
    hops[1] = hops[1] + part(left, 1)[...]
    made.append(far.start(hops.at[1], ins.at[1, 1], to(left)))
    return made


def reduce_kernel(
    total, wg, out, o0, o1, o2, o3, o4,
    f_hops, f_ins, f_mine, f_got, halves, acc, x_hops, x_ins, w1, y_hops, y_ins, w2, z_got, packed, send, recv,
):
    rep, zl, x, zh, y = place()
    other = device(1 - rep, zl, x, zh, y)

    def on_x(nx):
        return device(rep, zl, nx, zh, y)

    def on_y(ny):
        return device(rep, zl, x, zh, ny)

    zs = [(pair(zl, d) if d else zl, (1 - zh) if far_z else zh) for far_z in (0, 1) for d in range(4)][1:]
    ags = [((rep + dr) % 2, (y + dy) % 4) for dr in (0, 1) for dy in range(4)][1:]
    greet(
        [on_x((x + 1) % 4), on_x((x + 3) % 4)]
        + [device(rep, a, x, b, y) for a, b in zs]
        + [device(a, zl, x, zh, b) for a, b in ags]
    )
    far = Copies(send, recv)
    swaps = []
    xorder = [(x + 2) % 4, (x + 1) % 4, (x + 3) % 4, x]
    for nx in xorder:
        swaps.append(far.start(wg.at[:, nx, pl.ds(4 * (1 - rep), 4)], halves.at[:, nx], other))

    def f_part(ny, h):
        return total.at[:, ny, pl.ds(8 * h, 8)]

    f_first = ring_first(far, y, f_part, f_hops, on_y)

    def fold(i):
        swaps[i].wait_recv()
        nx = xorder[i]
        acc[:, nx] = wg[:, nx, pl.ds(4 * rep, 4)] + halves[:, nx]

    def x_part(nx, h):
        return acc.at[:, nx, pl.ds(2 * h, 2)]

    fold(0)
    x_first = ring_first(far, x, x_part, x_hops, on_x)
    fold(1)
    fold(2)
    f_rest = ring_rest(far, y, f_part, f_first, f_hops, f_ins, on_y)
    x_rest = ring_rest(far, x, x_part, x_first, x_hops, x_ins, on_x)
    fold(3)
    for copy in f_rest:
        copy.wait_recv()
    for h in range(2):
        at = pl.ds(8 * h, 8)
        f_mine[:, at] = total[:, y, at] + f_ins[0, h] + f_ins[1, h]
    f_swap = far.start(f_mine.at[1 - zh], f_got, device(rep, zl, x, 1 - zh, y))
    for copy in x_rest:
        copy.wait_recv()
    for h in range(2):
        at = pl.ds(2 * h, 2)
        w1[:, at] = acc[:, x, at] + x_ins[0, h] + x_ins[1, h]

    def y_part(ny, h):
        return w1.at[:, ny, pl.ds(40 * h, 40)]

    y_first = ring_first(far, y, y_part, y_hops, on_y)
    y_rest = ring_rest(far, y, y_part, y_first, y_hops, y_ins, on_y)
    for copy in y_rest:
        copy.wait_recv()
    for h in range(2):
        at = pl.ds(40 * h, 40)
        w2[:, at] = w1[:, y, at] + y_ins[0, h] + y_ins[1, h]
    z_made = [far.start(w2.at[a], z_got.at[i], device(rep, a, x, b, y)) for i, (a, b) in enumerate(zs)]
    f_swap.wait_recv()
    out[...] = f_mine[zh] + f_got[...]
    w3 = w2[zl]
    for i, copy in enumerate(z_made):
        copy.wait_recv()
        w3 = w3 + z_got[i]
    slot = rep * 4 + y
    packed[slot] = w3
    ag_made = [
        far.start(packed.at[slot], packed.at[slot], device(a, zl, x, zh, b)) for a, b in ags
    ]
    for copy in ag_made:
        copy.wait_recv()
    base, step = 0, packed.shape[1]
    for o in (o0, o1, o2, o3, o4):
        per = o.shape[0]
        for j in range(o.shape[1] // 128):
            done = 0
            while done < per:
                blk, off = (base + done) // step, (base + done) % step
                n = min(per - done, step - off)
                o[done : done + n, j * 128 : (j + 1) * 128] = packed[blk, off : off + n, :]
                done += n
            base += per
    far.drain()


def reduce(total, wg, weights, owners):
    feat = total.shape[1]
    chans = wg.shape[2]
    total = total.reshape(2, 4, 16, feat)
    wg = wg.reshape(4, 4, 8, PACK // 8, chans)
    q = PACK // 8
    vm = pl.BlockSpec(memory_space=pltpu.VMEM)
    count = 4 + 6 + 6 + 1 + 6 + 7 + 7
    outs = pl.pallas_call(
        reduce_kernel,
        out_shape=(
            jax.ShapeDtypeStruct((16, feat), F32),
            *[jax.ShapeDtypeStruct((w.shape[0] // owners, w.shape[1]), F32) for w in weights],
        ),
        in_specs=[vm, vm],
        out_specs=(vm,) * 6,
        scratch_shapes=[
            pltpu.VMEM((2, 2, 8, feat), F32),
            pltpu.VMEM((2, 2, 2, 8, feat), F32),
            pltpu.VMEM((2, 16, feat), F32),
            pltpu.VMEM((16, feat), F32),
            pltpu.VMEM((4, 4, 4, q, chans), F32),
            pltpu.VMEM((4, 4, 4, q, chans), F32),
            pltpu.VMEM((2, 4, 2, q, chans), F32),
            pltpu.VMEM((2, 2, 4, 2, q, chans), F32),
            pltpu.VMEM((4, 4, q, chans), F32),
            pltpu.VMEM((2, 4, q // 2, chans), F32),
            pltpu.VMEM((2, 2, 4, q // 2, chans), F32),
            pltpu.VMEM((4, q, chans), F32),
            pltpu.VMEM((7, q, chans), F32),
            pltpu.VMEM((8, q, chans), F32),
            pltpu.SemaphoreType.DMA((count,)),
            pltpu.SemaphoreType.DMA((count,)),
        ],
        compiler_params=pltpu.CompilerParams(
            collective_id=1, has_side_effects=True, vmem_limit_bytes=48 * 2**20
        ),
        name="gather_sums",
    )(total, wg)
    return outs


def local(src_feats, tgt_cotangent, rotation, edge_src, edge_tgt, edge_count, *weights):
    owners, n_tgt = lax.axis_size("src"), lax.axis_size("tgt")
    feat = src_feats.shape[2]
    xb, gb = gather(src_feats[0], tgt_cotangent[0], owners, n_tgt)
    total, wg = compute(
        xb.reshape(-1, feat), gb.reshape(-1, feat), rotation[0, 0, 0], edge_src[0, 0], edge_tgt[0, 0],
        edge_count[0, 0], weights, owners,
    )
    grad_feats, *grads = reduce(total, wg, weights, owners)
    return (grad_feats[None], *grads)


def solution(mesh):
    placed = (
        P("rep", ("src", "tgt"), None),
        P("rep", ("tgt", "src"), None),
        P("rep", "src", "tgt", None, None),
        P("rep", "src", "tgt", None),
        P("rep", "src", "tgt", None),
        P("rep", "src", "tgt"),
        P(), P(), P(), P(), P(),
    )
    return jax.shard_map(
        local,
        mesh=mesh,
        in_specs=placed,
        out_specs=(P("rep", ("src", "tgt"), None), *[P("src", None)] * 5),
        check_vma=False,
    )
```

```python
import jax
import jax.numpy as jnp
from jax import lax
from jax.experimental import pallas as pl
from jax.experimental.pallas import tpu as pltpu
from jax.sharding import PartitionSpec as P

OFFSETS = (0, 1, 10, 35, 70)
F32, BF16 = jnp.float32, jnp.bfloat16
MESH = pl.DeviceIdType.MESH
PACK = 640
NT = (((1,), (1,)), ((), ()))
NN = (((1,), (0,)), ((), ()))


def mm(a, b, dims):
    return lax.dot_general(a, b, dims, preferred_element_type=F32)


def split(a):
    hi = a.astype(BF16)
    return hi, (a - hi.astype(F32)).astype(BF16)


def onehot(ids, live, atoms):
    rows = lax.broadcasted_iota(jnp.int32, (atoms, ids.shape[1]), 0)
    return jnp.where((rows == ids) & live, 1.0, 0.0).astype(BF16)


def place():
    rep, src, tgt = lax.axis_index("rep"), lax.axis_index("src"), lax.axis_index("tgt")
    return rep, src // 4, src % 4, tgt // 4, tgt % 4


def device(rep, zl, x, zh, y):
    return (rep, zl * 4 + x, zh * 4 + y)


def pair(i, d):
    return (i + 1 - 2 * (i % 2), (i + 2) % 4, 3 - i)[d - 1]


class Copies:
    def __init__(self, send, recv):
        self.send, self.recv, self.made = send, recv, []

    def start(self, src, dst, to):
        n = len(self.made)
        copy = pltpu.make_async_remote_copy(
            src_ref=src, dst_ref=dst, send_sem=self.send.at[n], recv_sem=self.recv.at[n],
            device_id=to, device_id_type=MESH,
        )
        copy.start()
        self.made.append(copy)
        return copy

    def drain(self):
        for copy in self.made:
            copy.wait_send()


def greet(peers):
    barrier = pltpu.get_barrier_semaphore()
    for peer in peers:
        pl.semaphore_signal(barrier, inc=1, device_id=peer, device_id_type=MESH)
    pl.semaphore_wait(barrier, len(peers))


def ring_first(far, me, part, hops, to):
    right, left, opp = (me + 1) % 4, (me + 3) % 4, (me + 2) % 4
    return (
        far.start(part(opp, 0), hops.at[0], to(right)),
        far.start(part(opp, 1), hops.at[1], to(left)),
    )


def ring_own(far, me, part, ins, to):
    right, left = (me + 1) % 4, (me + 3) % 4
    return [
        far.start(part(right, 1), ins.at[0, 1], to(right)),
        far.start(part(left, 0), ins.at[1, 0], to(left)),
    ]


def ring_rest(far, me, part, firsts, hops, ins, to):
    right, left = (me + 1) % 4, (me + 3) % 4
    made = []
    firsts[0].wait_recv()
    hops[0] = hops[0] + part(right, 0)[...]
    made.append(far.start(hops.at[0], ins.at[0, 0], to(right)))
    firsts[1].wait_recv()
    hops[1] = hops[1] + part(left, 1)[...]
    made.append(far.start(hops.at[1], ins.at[1, 1], to(left)))
    return made


def pick(block_ref, hot_ref, out_ref, first, width, count):
    def one(i, carry):
        at = pl.multiple_of(first + i * width, 128)
        block = block_ref[:, :, pl.ds(at, width)]
        hi, lo = split(block.reshape(-1, width).T)
        out_ref[pl.ds(at, width), :] = mm(jnp.concatenate([hi, lo], 1), hot_ref[...], NN)
        return carry

    lax.fori_loop(0, count, one, 0)


def rotate(rows_ref, rot_ref, put, chans, cap, levels):
    steps, lanes = 16, 128
    tiles = cap // lanes

    def one(i, carry):
        ch = pl.multiple_of((i // tiles) * steps, steps)
        ln = pl.multiple_of((i % tiles) * lanes, lanes)
        for level in levels:
            q, cols = min(level, 2), 2 * level + 1
            xs = [
                rows_ref[pl.ds((level * level + c) * chans + ch, steps), pl.ds(ln, lanes)]
                for c in range(cols)
            ]
            for r in range(2 * q + 1):
                acc = None
                for c in range(cols):
                    o = OFFSETS[level] + r * cols + c
                    term = rot_ref[o, :, pl.ds(ln, lanes)] * xs[c]
                    acc = term if acc is None else acc + term
                m = r - q
                put(abs(m), m < 0, level - abs(m), ch, ln, acc)
        return carry

    lax.fori_loop(0, (chans // steps) * tiles, one, 0)


def pieces(first, count, step):
    done = 0
    while done < count:
        blk, off = (first + done) // step, (first + done) % step
        n = min(count - done, step - off)
        yield blk, off, done, n
        done += n


def tile_kernel(
    cnt_ref, es_ref, et_ref, x_in, g_in, rot_in, w0_in, w1r_in, w1i_in, w2r_in, w2i_in,
    out, packed,
    rot_ref, wf0, wf1r, wf1i, wf2r, wf2i, wh0, wh1r, wh1i, wh2r, wh2i,
    x_ref, g_ref, hs_ref, ht_ref, hs2_ref, rows_ref,
    z0_ref, z1_ref, z2_ref, u0_ref, u1_ref, u2_ref, v1_ref, v2_ref, term_ref,
    total, wg, f_hops, f_ins, f_mine, f_got, halves, x_hops, x_ins, w1, y_hops, y_ins, w2, z_got,
    send, recv, own,
):
    rep, zl, x, zh, y = place()
    cap, chans, feat = es_ref.shape[1], 128, x_in.shape[1]
    src_blk, tgt_blk = hs_ref.shape[0] // 2, ht_ref.shape[0] // 2
    owned = [
        pltpu.make_async_copy(a, b, own.at[i])
        for i, (a, b) in enumerate(
            ((w0_in, wf0), (w1r_in, wf1r), (w1i_in, wf1i), (w2r_in, wf2r), (w2i_in, wf2i), (rot_in, rot_ref))
        )
    ]

    right, left = (x + 1) % 4, (x + 3) % 4
    up, down = (y + 1) % 4, (y + 3) % 4
    zs = [(pair(zl, d) if d else zl, (1 - zh) if far_z else zh) for far_z in (0, 1) for d in range(4)][1:]
    ags = [((rep + dr) % 2, (y + dy) % 4) for dr in (0, 1) for dy in range(4)][1:]
    lines = [pair(zl, d) for d in (1, 2, 3)]
    across, other = device(rep, zl, x, 1 - zh, y), device(1 - rep, zl, x, zh, y)

    def on_x(nx):
        return device(rep, zl, nx, zh, y)

    def on_y(ny):
        return device(rep, zl, x, zh, ny)

    def on_z(nz):
        return device(rep, nz, x, zh, y)

    greet(
        [on_x(left), on_x(right)]
        + [device(rep, a, x, b, y) for a, b in zs]
        + [device(a, zl, x, zh, b) for a, b in ags]
    )
    far = Copies(send, recv)

    mine_g, mine_x = zl * 4 + x, zh * 4 + y
    parts = (pl.ds(0, 16 * chans), pl.ds(16 * chans, 9 * chans))
    whole = pl.ds(0, feat)

    def both(src, slot, at, out_ref, to, one, two):
        dst = out_ref.at[slot, :, at]
        return far.start(src, dst, to(one)), far.start(src, dst, to(two))

    def relay(copies, out_ref, at, slots, to, one, two):
        copies[0].wait_recv()
        ref = out_ref.at[slots[0], :8, at]
        a = far.start(ref, ref, to(one))
        copies[1].wait_recv()
        ref = out_ref.at[slots[1], 8:, at]
        return a, far.start(ref, ref, to(two))

    z_go = [None, None]
    xs, ends_g, ends_x, ys = ([], []), ([], []), [], []

    def z_start(p):
        at = parts[p]
        z_go[p] = [far.start(g_in.at[:, at], g_ref.at[mine_g, :, at], on_z(n)) for n in lines]

    z_start(0)
    hop = far.start(x_in, x_ref.at[mine_x], across)
    xs[0].append(both(g_in.at[:, parts[0]], mine_g, parts[0], g_ref, on_x, right, left))
    ys.append(both(x_in, mine_x, whole, x_ref, on_y, up, down))
    z_start(1)
    xs[1].append(both(g_in.at[:, parts[1]], mine_g, parts[1], g_ref, on_x, right, left))
    owned.append(pltpu.make_async_copy(g_in, g_ref.at[mine_g], own.at[6]))
    owned.append(pltpu.make_async_copy(x_in, x_ref.at[mine_x], own.at[7]))
    for copy in owned:
        copy.start()
    order = [zl, *lines]

    def x_step(p, j):
        z_go[p][j - 1].wait_recv()
        slot = order[j] * 4 + x
        xs[p].append(both(g_ref.at[slot, :, parts[p]], slot, parts[p], g_ref, on_x, right, left))

    def x_relay(p, j):
        slots = (order[j] * 4 + left, order[j] * 4 + right)
        ends_g[p].extend(relay(xs[p][j], g_ref, parts[p], slots, on_x, right, left))

    def y_relay(j):
        at = (zh, 1 - zh)[j] * 4
        ends_x.extend(relay(ys[j], x_ref, whole, (at + down, at + up), on_y, up, down))

    live = lax.broadcasted_iota(jnp.int32, (1, cap), 1) < cnt_ref[0]
    hot = onehot(es_ref[...], live, src_blk)
    hs_ref[:src_blk, :] = hot
    hs_ref[src_blk:, :] = hot
    hs2_ref[:, :cap] = hot
    hs2_ref[:, cap:] = hot
    hot = onehot(et_ref[...], live, tgt_blk)
    ht_ref[:tgt_blk, :] = hot
    ht_ref[tgt_blk:, :] = hot
    for copy in owned:
        copy.wait()
    for src, dst in ((wf0, wh0), (wf1r, wh1r), (wf1i, wh1i), (wf2r, wh2r), (wf2i, wh2i)):
        def cut(i, carry, src=src, dst=dst):
            at = pl.ds(pl.multiple_of(i * 128, 128), 128)
            dst[0, at, :], dst[1, at, :] = split(src[at, :])
            return carry

        lax.fori_loop(0, src.shape[0] // 128, cut, 0)

    x_step(0, 1)
    x_relay(0, 0)
    y_relay(0)
    x_step(0, 2)
    x_relay(0, 1)
    hop.wait_recv()
    slot = (1 - zh) * 4 + y
    ys.append(both(x_ref.at[slot], slot, whole, x_ref, on_y, up, down))
    x_step(0, 3)
    x_relay(0, 2)
    y_relay(1)
    x_step(1, 1)
    x_relay(0, 3)
    x_relay(1, 0)
    x_step(1, 2)
    for copy in ends_x:
        copy.wait_recv()

    zrefs = (z0_ref, z1_ref, z2_ref)

    def put_z(order, neg, k, ch, ln, val):
        hi, lo = split(val)
        rows = pl.ds(k * chans + ch, 16)
        at = pl.ds(ln + (cap if neg else 0), 128)
        zrefs[order][0, rows, at] = hi
        zrefs[order][1, rows, at] = lo

    pick(x_ref, hs_ref, rows_ref, 0, 5 * chans, 5)
    x_relay(1, 1)
    x_step(1, 3)
    x_relay(1, 2)
    rotate(rows_ref, rot_ref, put_z, chans, cap, range(5))
    x_relay(1, 3)

    urefs = (u0_ref, u1_ref, u2_ref)
    vrefs = (None, v1_ref, v2_ref)

    def put_u(order, neg, k, ch, ln, val):
        hi, lo = split(val)
        rows = pl.ds(k * chans + ch, 16)
        at = pl.ds(ln + (cap if neg else 0), 128)
        urefs[order][0, rows, at] = hi
        urefs[order][1, rows, at] = lo
        if order:
            at = pl.ds(ln + (0 if neg else cap), 128)
            vrefs[order][0, rows, at] = hi if neg else -hi
            vrefs[order][1, rows, at] = lo if neg else -lo

    for copy in ends_g[0]:
        copy.wait_recv()
    pick(g_ref, ht_ref, rows_ref, 0, 4 * chans, 4)
    rotate(rows_ref, rot_ref, put_u, chans, cap, range(4))
    for copy in ends_g[1]:
        copy.wait_recv()
    pick(g_ref, ht_ref, rows_ref, 16 * chans, 3 * chans, 3)
    rotate(rows_ref, rot_ref, put_u, chans, cap, (4,))

    def grad(z, u, at, count):
        zhi, zlo = z[0, pl.ds(at, count), :], z[1, pl.ds(at, count), :]
        return mm(zhi, u[0], NT) + mm(zhi, u[1], NT) + mm(zlo, u[0], NT)

    quarter = wg.shape[3]
    xorder = [(x + 2) % 4, right, left, x]
    swaps = []
    for h in range(2):
        base = 0
        for zr, ur, cols in (
            (z0_ref, u0_ref, 5), (z1_ref, u1_ref, 4), (z1_ref, v1_ref, 4), (z2_ref, u2_ref, 3), (z2_ref, v2_ref, 3),
        ):
            per = cols * chans // 16
            res = grad(zr, ur, h * 8 * per, 8 * per)
            for s in range(8):
                for j in range(cols):
                    for blk, off, done, n in pieces(base + j * per, per, quarter):
                        wg[2 * h + s // 4, s % 4, blk, off : off + n, :] = res[
                            s * per + done : s * per + done + n, j * chans : (j + 1) * chans
                        ]
            base += cols * per
        for blk, off, done, n in pieces(base, 8 * quarter - base, quarter):
            wg[2 * h : 2 * h + 2, :, blk, off : off + n, :] = jnp.zeros((2, 4, n, chans), F32)
        for nx in xorder:
            zz = pl.ds(2 * h, 2)
            swaps.append(far.start(wg.at[zz, nx, pl.ds(4 * (1 - rep), 4)], halves.at[zz, nx], other))

    def three(w, u):
        return mm(w[0], u[0], NN) + mm(w[0], u[1], NN) + mm(w[1], u[0], NN)

    firsts = (0, 5 * chans, 13 * chans)

    def keep(order, res):
        rows = res.shape[0]
        rows_ref[firsts[order] : firsts[order] + rows, :] = res[:, :cap]
        if order:
            rows_ref[firsts[order] + rows : firsts[order] + 2 * rows, :] = res[:, cap:]

    def fold(i):
        swaps[i].wait_recv()
        swaps[4 + i].wait_recv()
        nx = xorder[i]
        halves[:, nx] = wg[:, nx, pl.ds(4 * rep, 4)] + halves[:, nx]

    def x_part(nx, h):
        return halves.at[:, nx, pl.ds(2 * h, 2)]

    keep(0, three(wh0, u0_ref))
    keep(2, three(wh2r, u2_ref) + three(wh2i, v2_ref))
    fold(0)
    x_first = ring_first(far, x, x_part, x_hops, on_x)
    fold(1)
    fold(2)
    x_rest = ring_own(far, x, x_part, x_ins, on_x)
    fold(3)
    keep(1, three(wh1r, u1_ref) + three(wh1i, v1_ref))
    x_rest += ring_rest(far, x, x_part, x_first, x_hops, x_ins, on_x)

    tiles = cap // 128

    def back(i, carry):
        ch = pl.multiple_of((i // tiles) * 16, 16)
        ln = pl.multiple_of((i % tiles) * 128, 128)
        for level in range(5):
            q, cols = min(level, 2), 2 * level + 1
            ds = []
            for r in range(2 * q + 1):
                m = r - q
                k = level - abs(m) + (((5 - abs(m)) if m < 0 else 0))
                ds.append(rows_ref[pl.ds(firsts[abs(m)] + k * chans + ch, 16), pl.ds(ln, 128)])
            for c in range(cols):
                acc = None
                for r in range(2 * q + 1):
                    o = OFFSETS[level] + r * cols + c
                    term = rot_ref[o, :, pl.ds(ln, 128)] * ds[r]
                    acc = term if acc is None else acc + term
                hi, lo = split(acc)
                rows = pl.ds((level * level + c) * chans + ch, 16)
                term_ref[rows, pl.ds(ln, 128)] = hi
                term_ref[rows, pl.ds(ln + cap, 128)] = lo
        return carry

    lax.fori_loop(0, (chans // 16) * tiles, back, 0)

    def scatter(c, carry):
        at = pl.multiple_of(c * 5 * chans, chans)
        res = mm(hs2_ref[...], term_ref[pl.ds(at, 5 * chans), :], NT)
        total[:, :, :, pl.ds(at, 5 * chans)] = res.reshape(2, 4, 16, 5 * chans)
        return carry

    lax.fori_loop(0, 5, scatter, 0)

    def f_part(ny, h):
        return total.at[:, ny, pl.ds(8 * h, 8)]

    f_first = ring_first(far, y, f_part, f_hops, on_y)
    f_rest = ring_own(far, y, f_part, f_ins, on_y)
    for copy in x_rest:
        copy.wait_recv()
    for h in range(2):
        at = pl.ds(2 * h, 2)
        w1[:, at] = halves[:, x, at] + x_ins[0, h] + x_ins[1, h]

    def y_part(ny, h):
        return w1.at[:, ny, pl.ds(40 * h, 40)]

    y_first = ring_first(far, y, y_part, y_hops, on_y)
    f_rest += ring_rest(far, y, f_part, f_first, f_hops, f_ins, on_y)
    y_rest = ring_own(far, y, y_part, y_ins, on_y)
    y_rest += ring_rest(far, y, y_part, y_first, y_hops, y_ins, on_y)
    for copy in f_rest:
        copy.wait_recv()
    for h in range(2):
        at = pl.ds(8 * h, 8)
        f_mine[:, at] = total[:, y, at] + f_ins[0, h] + f_ins[1, h]
    f_swap = far.start(f_mine.at[1 - zh], f_got, across)
    for copy in y_rest:
        copy.wait_recv()
    for h in range(2):
        at = pl.ds(40 * h, 40)
        w2[:, at] = w1[:, y, at] + y_ins[0, h] + y_ins[1, h]
    z_made = [far.start(w2.at[a], z_got.at[i], device(rep, a, x, b, y)) for i, (a, b) in enumerate(zs)]
    w3 = w2[zl]
    for i, copy in enumerate(z_made):
        copy.wait_recv()
        w3 = w3 + z_got[i]
    slot = rep * 4 + y
    packed[slot] = w3
    ag_made = [
        far.start(packed.at[slot], packed.at[slot], device(a, zl, x, zh, b)) for a, b in ags
    ]
    f_swap.wait_recv()
    out[...] = f_mine[zh] + f_got[...]
    for copy in ag_made:
        copy.wait_recv()
    far.drain()


def finish_kernel(feats, packed, out, o0, o1, o2, o3, o4):
    out[...] = feats[...]
    base = 0
    for o in (o0, o1, o2, o3, o4):
        per = o.shape[0]
        for j in range(o.shape[1] // 128):
            for blk, off, done, n in pieces(base, per, packed.shape[1]):
                o[done : done + n, j * 128 : (j + 1) * 128] = packed[blk, off : off + n, :]
            base += per


def run(src_feats, tgt_cotangent, wig, es, et, cnt, weights, owners, n_tgt):
    cap = es.shape[1]
    chans = 128
    rows, feat = src_feats.shape
    src_blk, tgt_blk = n_tgt * rows, owners * rows
    q = PACK // 8
    vm = pl.BlockSpec(memory_space=pltpu.VMEM)
    anywhere = pl.BlockSpec(memory_space=pl.ANY)
    dims = [w.shape[0] for w in weights]
    count = 2 * 19 + 9 + 8 + 6 + 6 + 1 + 6 + 7 + 7
    feats, packed = pl.pallas_call(
        tile_kernel,
        out_shape=(
            jax.ShapeDtypeStruct((rows, feat), F32),
            jax.ShapeDtypeStruct((8, q, chans), F32),
        ),
        in_specs=[pl.BlockSpec(memory_space=pltpu.SMEM), vm, vm] + [anywhere] * 8,
        out_specs=(vm, vm),
        scratch_shapes=[
            pltpu.VMEM(wig.shape, F32),
            *[pltpu.VMEM((d, d), F32) for d in dims],
            *[pltpu.VMEM((2, d, d), BF16) for d in dims],
            pltpu.VMEM((n_tgt, rows, feat), F32),
            pltpu.VMEM((owners, rows, feat), F32),
            pltpu.VMEM((2 * src_blk, cap), BF16),
            pltpu.VMEM((2 * tgt_blk, cap), BF16),
            pltpu.VMEM((src_blk, 2 * cap), BF16),
            pltpu.VMEM((feat, cap), F32),
            pltpu.VMEM((2, dims[0], cap), BF16),
            pltpu.VMEM((2, dims[1], 2 * cap), BF16),
            pltpu.VMEM((2, dims[3], 2 * cap), BF16),
            pltpu.VMEM((2, dims[0], cap), BF16),
            pltpu.VMEM((2, dims[1], 2 * cap), BF16),
            pltpu.VMEM((2, dims[3], 2 * cap), BF16),
            pltpu.VMEM((2, dims[1], 2 * cap), BF16),
            pltpu.VMEM((2, dims[3], 2 * cap), BF16),
            pltpu.VMEM((feat, 2 * cap), BF16),
            pltpu.VMEM((2, 4, rows, feat), F32),
            pltpu.VMEM((4, 4, 8, q, chans), F32),
            pltpu.VMEM((2, 2, 8, feat), F32),
            pltpu.VMEM((2, 2, 2, 8, feat), F32),
            pltpu.VMEM((2, rows, feat), F32),
            pltpu.VMEM((rows, feat), F32),
            pltpu.VMEM((4, 4, 4, q, chans), F32),
            pltpu.VMEM((2, 4, 2, q, chans), F32),
            pltpu.VMEM((2, 2, 4, 2, q, chans), F32),
            pltpu.VMEM((4, 4, q, chans), F32),
            pltpu.VMEM((2, 4, q // 2, chans), F32),
            pltpu.VMEM((2, 2, 4, q // 2, chans), F32),
            pltpu.VMEM((4, q, chans), F32),
            pltpu.VMEM((7, q, chans), F32),
            pltpu.SemaphoreType.DMA((count,)),
            pltpu.SemaphoreType.DMA((count,)),
            pltpu.SemaphoreType.DMA((8,)),
        ],
        compiler_params=pltpu.CompilerParams(
            collective_id=0, has_side_effects=True, vmem_limit_bytes=62 * 2**20
        ),
        name="tile",
    )(cnt, es, et, src_feats, tgt_cotangent, wig, *weights)
    return pl.pallas_call(
        finish_kernel,
        out_shape=(
            jax.ShapeDtypeStruct((rows, feat), F32),
            *[jax.ShapeDtypeStruct((d // owners, d), F32) for d in dims],
        ),
        in_specs=[vm, vm],
        out_specs=(vm,) * 6,
        name="finish",
    )(feats, packed)


def local(src_feats, tgt_cotangent, rotation, edge_src, edge_tgt, edge_count, *weights):
    wig = rotation.transpose(0, 1, 3, 2, 4)[0, 0]
    grad_feats, *grads = run(
        src_feats[0], tgt_cotangent[0], wig, edge_src[0, 0], edge_tgt[0, 0], edge_count[0, 0], weights,
        lax.axis_size("src"), lax.axis_size("tgt"),
    )
    return (grad_feats[None], *grads)


def solution(mesh):
    placed = (
        P("rep", ("src", "tgt"), None),
        P("rep", ("tgt", "src"), None),
        P("rep", "src", "tgt", None, None),
        P("rep", "src", "tgt", None),
        P("rep", "src", "tgt", None),
        P("rep", "src", "tgt"),
        P(), P(), P(), P(), P(),
    )
    return jax.shard_map(
        local,
        mesh=mesh,
        in_specs=placed,
        out_specs=(P("rep", ("src", "tgt"), None), *[P("src", None)] * 5),
        check_vma=False,
    )
```

```python
import functools

import jax
import jax.numpy as jnp
from jax import lax
from jax.experimental import pallas as pl
from jax.experimental.pallas import tpu as pltpu
from jax.sharding import PartitionSpec as P

OFFSETS = (0, 1, 10, 35, 70)
F32, BF16 = jnp.float32, jnp.bfloat16
MESH = pl.DeviceIdType.MESH
PACK = 640
NT = (((1,), (1,)), ((), ()))
NN = (((1,), (0,)), ((), ()))


def mm(a, b, dims):
    return lax.dot_general(a, b, dims, preferred_element_type=F32)


def split(a):
    hi = a.astype(BF16)
    return hi, (a - hi.astype(F32)).astype(BF16)


def onehot(ids, live, atoms):
    rows = lax.broadcasted_iota(jnp.int32, (atoms, ids.shape[1]), 0)
    return jnp.where((rows == ids) & live, 1.0, 0.0).astype(BF16)


def place():
    rep, src, tgt = lax.axis_index("rep"), lax.axis_index("src"), lax.axis_index("tgt")
    return rep, src // 4, src % 4, tgt // 4, tgt % 4


def device(rep, zl, x, zh, y):
    return (rep, zl * 4 + x, zh * 4 + y)


def pair(i, d):
    return (i + 1 - 2 * (i % 2), (i + 2) % 4, 3 - i)[d - 1]


class Copies:
    def __init__(self, send, recv):
        self.send, self.recv, self.made = send, recv, []

    def start(self, src, dst, to):
        n = len(self.made)
        copy = pltpu.make_async_remote_copy(
            src_ref=src, dst_ref=dst, send_sem=self.send.at[n], recv_sem=self.recv.at[n],
            device_id=to, device_id_type=MESH,
        )
        copy.start()
        self.made.append(copy)
        return copy

    def drain(self):
        for copy in self.made:
            copy.wait_send()


def greet(peers):
    barrier = pltpu.get_barrier_semaphore()
    for peer in peers:
        pl.semaphore_signal(barrier, inc=1, device_id=peer, device_id_type=MESH)
    pl.semaphore_wait(barrier, len(peers))


def ring_first(far, me, part, hops, to):
    right, left, opp = (me + 1) % 4, (me + 3) % 4, (me + 2) % 4
    return (
        far.start(part(opp, 0), hops.at[0], to(right)),
        far.start(part(opp, 1), hops.at[1], to(left)),
    )


def ring_own(far, me, part, ins, to):
    right, left = (me + 1) % 4, (me + 3) % 4
    return [
        far.start(part(right, 1), ins.at[0, 1], to(right)),
        far.start(part(left, 0), ins.at[1, 0], to(left)),
    ]


def ring_rest(far, me, part, firsts, hops, ins, to):
    right, left = (me + 1) % 4, (me + 3) % 4
    made = []
    firsts[0].wait_recv()
    hops[0] = hops[0] + part(right, 0)[...]
    made.append(far.start(hops.at[0], ins.at[0, 0], to(right)))
    firsts[1].wait_recv()
    hops[1] = hops[1] + part(left, 1)[...]
    made.append(far.start(hops.at[1], ins.at[1, 1], to(left)))
    return made


def pick(block_ref, hot_ref, out_ref, first, width, count):
    def one(i, carry):
        at = pl.multiple_of(first + i * width, 128)
        block = block_ref[:, :, pl.ds(at, width)]
        hi, lo = split(block.reshape(-1, width).T)
        out_ref[pl.ds(at, width), :] = mm(jnp.concatenate([hi, lo], 1), hot_ref[...], NN)
        return carry

    lax.fori_loop(0, count, one, 0)


def rotate(rows_ref, rot_ref, put, chans, cap, levels):
    steps, lanes = 16, 128
    tiles = cap // lanes

    def one(i, carry):
        ch = pl.multiple_of((i // tiles) * steps, steps)
        ln = pl.multiple_of((i % tiles) * lanes, lanes)
        for level in levels:
            q, cols = min(level, 2), 2 * level + 1
            xs = [
                rows_ref[pl.ds((level * level + c) * chans + ch, steps), pl.ds(ln, lanes)]
                for c in range(cols)
            ]
            for r in range(2 * q + 1):
                acc = None
                for c in range(cols):
                    o = OFFSETS[level] + r * cols + c
                    term = rot_ref[o, :, pl.ds(ln, lanes)] * xs[c]
                    acc = term if acc is None else acc + term
                m = r - q
                put(abs(m), m < 0, level - abs(m), ch, ln, acc)
        return carry

    lax.fori_loop(0, (chans // steps) * tiles, one, 0)


def pieces(first, count, step):
    done = 0
    while done < count:
        blk, off = (first + done) // step, (first + done) % step
        n = min(count - done, step - off)
        yield blk, off, done, n
        done += n


def tile_kernel(
    cnt_ref, es_ref, et_ref, x_in, g_in, rot_in, w0_in, w1r_in, w1i_in, w2r_in, w2i_in,
    out, packed,
    rot_ref, wf0, wf1r, wf1i, wf2r, wf2i, wh0, wh1r, wh1i, wh2r, wh2i,
    x_ref, g_ref, hs_ref, ht_ref, hs2_ref, rows_ref,
    z0_ref, z1_ref, z2_ref, u0_ref, u1_ref, u2_ref, v1_ref, v2_ref, term_ref,
    total, wg, f_hops, f_ins, f_mine, f_got, halves, a_hops, a_ins, b_hops, b_ins,
    wa, wb, a2_hops, a2_ins, b2_hops, b2_ins, w2, z_got,
    send, recv, line_send, line_recv, own,
):
    rep, zl, x, zh, y = place()
    cap, chans, feat = es_ref.shape[1], 128, x_in.shape[1]
    src_blk, tgt_blk = hs_ref.shape[0] // 2, ht_ref.shape[0] // 2
    owned = [
        pltpu.make_async_copy(a, b, own.at[i])
        for i, (a, b) in enumerate(
            ((w0_in, wf0), (w1r_in, wf1r), (w1i_in, wf1i), (w2r_in, wf2r), (w2i_in, wf2i), (rot_in, rot_ref))
        )
    ]

    right, left = (x + 1) % 4, (x + 3) % 4
    up, down = (y + 1) % 4, (y + 3) % 4
    zs = [(pair(zl, d) if d else zl, (1 - zh) if far_z else zh) for far_z in (0, 1) for d in range(4)][1:]
    ags = [((rep + dr) % 2, (y + dy) % 4) for dr in (0, 1) for dy in range(4)][1:]
    inner = ((zl + 1) // 2) % 2 == 1
    mate, inward, beyond = pair(zl, 1), 2 - zl // 2, 3 - 3 * (zl // 2)
    across, other = device(rep, zl, x, 1 - zh, y), device(1 - rep, zl, x, zh, y)

    def on_x(nx):
        return device(rep, zl, nx, zh, y)

    def on_y(ny):
        return device(rep, zl, x, zh, ny)

    def on_z(nz):
        return device(rep, nz, x, zh, y)

    greet(
        [on_x(left), on_x(right)]
        + [device(rep, a, x, b, y) for a, b in zs]
        + [device(a, zl, x, zh, b) for a, b in ags]
    )
    far = Copies(send, recv)

    mine_g, mine_x = zl * 4 + x, zh * 4 + y
    parts = (pl.ds(0, 16 * chans), pl.ds(16 * chans, 9 * chans))
    whole = pl.ds(0, feat)

    def both(src, slot, at, out_ref, to, one, two):
        dst = out_ref.at[slot, :, at]
        return far.start(src, dst, to(one)), far.start(src, dst, to(two))

    def relay(copies, out_ref, at, slots, to, one, two):
        copies[0].wait_recv()
        ref = out_ref.at[slots[0], :8, at]
        a = far.start(ref, ref, to(one))
        copies[1].wait_recv()
        ref = out_ref.at[slots[1], 8:, at]
        return a, far.start(ref, ref, to(two))

    xs, ends_g, ends_x, ys = ([], []), ([], []), [], []
    order = [zl, mate, inward, beyond]

    def hand(p, who, sent, got, to):
        dst = g_ref.at[who * 4 + x, :, parts[p]]
        return pltpu.make_async_remote_copy(
            src_ref=g_in.at[:, parts[p]] if who is zl else dst, dst_ref=dst,
            send_sem=line_send.at[5 * p + sent], recv_sem=line_recv.at[3 * p + got],
            device_id=on_z(to), device_id_type=MESH,
        )

    def line_start(p):
        hand(p, zl, 0, 0, mate).start()

        @pl.when(inner)
        def _():
            hand(p, zl, 1, 1, inward).start()

    def line_next(p, k):
        hand(p, order[k + 1], 0, k, mate).wait_recv()

        @pl.when(inner)
        def _():
            if k == 0:
                hand(p, mate, 2, 2, inward).start()
            elif k == 1:
                hand(p, inward, 3, 1, mate).start()
            else:
                hand(p, beyond, 4, 2, mate).start()

    def line_drain(p):
        hand(p, zl, 0, 0, mate).wait_send()

        @pl.when(inner)
        def _():
            for k in range(1, 5):
                hand(p, zl, k, 0, mate).wait_send()

    line_start(0)
    xs[0].append(both(g_in.at[:, parts[0]], mine_g, parts[0], g_ref, on_x, right, left))
    ys.append(both(x_in, mine_x, whole, x_ref, on_y, up, down))
    xs[1].append(both(g_in.at[:, parts[1]], mine_g, parts[1], g_ref, on_x, right, left))
    owned.append(pltpu.make_async_copy(g_in, g_ref.at[mine_g], own.at[6]))
    owned.append(pltpu.make_async_copy(x_in, x_ref.at[mine_x], own.at[7]))
    for copy in owned:
        copy.start()

    def x_step(p, j):
        line_next(p, j - 1)
        slot = order[j] * 4 + x
        xs[p].append(both(g_ref.at[slot, :, parts[p]], slot, parts[p], g_ref, on_x, right, left))

    def x_relay(p, j):
        slots = (order[j] * 4 + left, order[j] * 4 + right)
        ends_g[p].extend(relay(xs[p][j], g_ref, parts[p], slots, on_x, right, left))

    def y_relay(j):
        at = (zh, 1 - zh)[j] * 4
        ends_x.extend(relay(ys[j], x_ref, whole, (at + down, at + up), on_y, up, down))

    live = lax.broadcasted_iota(jnp.int32, (1, cap), 1) < cnt_ref[0]
    hot = onehot(es_ref[...], live, src_blk)
    hs_ref[:src_blk, :] = hot
    hs_ref[src_blk:, :] = hot
    hs2_ref[:, :cap] = hot
    hs2_ref[:, cap:] = hot
    hot = onehot(et_ref[...], live, tgt_blk)
    ht_ref[:tgt_blk, :] = hot
    ht_ref[tgt_blk:, :] = hot
    for copy in owned:
        copy.wait()
    for src, dst in ((wf0, wh0), (wf1r, wh1r), (wf1i, wh1i), (wf2r, wh2r), (wf2i, wh2i)):
        def cut(i, carry, src=src, dst=dst):
            at = pl.ds(pl.multiple_of(i * 128, 128), 128)
            dst[0, at, :], dst[1, at, :] = split(src[at, :])
            return carry

        lax.fori_loop(0, src.shape[0] // 128, cut, 0)

    x_step(0, 1)
    hop = far.start(x_in, x_ref.at[mine_x], across)
    x_relay(0, 0)
    x_step(0, 2)
    line_start(1)
    x_relay(0, 1)
    y_relay(0)
    x_step(0, 3)
    x_relay(0, 2)
    hop.wait_recv()
    slot = (1 - zh) * 4 + y
    ys.append(both(x_ref.at[slot], slot, whole, x_ref, on_y, up, down))
    x_step(1, 1)
    x_relay(0, 3)
    x_relay(1, 0)
    x_step(1, 2)
    y_relay(1)
    x_relay(1, 1)

    zrefs = (z0_ref, z1_ref, z2_ref)

    def put_z(order, neg, k, ch, ln, val):
        hi, lo = split(val)
        rows = pl.ds(k * chans + ch, 16)
        at = pl.ds(ln + (cap if neg else 0), 128)
        zrefs[order][0, rows, at] = hi
        zrefs[order][1, rows, at] = lo

    x_step(1, 3)
    for copy in ends_x:
        copy.wait_recv()
    pick(x_ref, hs_ref, rows_ref, 0, 5 * chans, 5)
    x_relay(1, 2)
    x_relay(1, 3)
    rotate(rows_ref, rot_ref, put_z, chans, cap, range(5))

    urefs = (u0_ref, u1_ref, u2_ref)
    vrefs = (None, v1_ref, v2_ref)

    def put_u(order, neg, k, ch, ln, val):
        hi, lo = split(val)
        rows = pl.ds(k * chans + ch, 16)
        at = pl.ds(ln + (cap if neg else 0), 128)
        urefs[order][0, rows, at] = hi
        urefs[order][1, rows, at] = lo
        if order:
            at = pl.ds(ln + (0 if neg else cap), 128)
            vrefs[order][0, rows, at] = hi if neg else -hi
            vrefs[order][1, rows, at] = lo if neg else -lo

    for copy in ends_g[0]:
        copy.wait_recv()
    pick(g_ref, ht_ref, rows_ref, 0, 4 * chans, 4)
    rotate(rows_ref, rot_ref, put_u, chans, cap, range(4))
    for copy in ends_g[1]:
        copy.wait_recv()
    pick(g_ref, ht_ref, rows_ref, 16 * chans, 3 * chans, 3)
    rotate(rows_ref, rot_ref, put_u, chans, cap, (4,))

    def grad(z, u, at, count):
        zhi, zlo = z[0, pl.ds(at, count), :], z[1, pl.ds(at, count), :]
        return mm(zhi, u[0], NT) + mm(zhi, u[1], NT) + mm(zlo, u[0], NT)

    quarter = wg.shape[3]
    xorder = [(x + 2) % 4, right, left, x]
    swaps = []
    for h in range(2):
        base = 0
        for zr, ur, cols in (
            (z0_ref, u0_ref, 5), (z1_ref, u1_ref, 4), (z1_ref, v1_ref, 4), (z2_ref, u2_ref, 3), (z2_ref, v2_ref, 3),
        ):
            per = cols * chans // 16
            res = grad(zr, ur, h * 8 * per, 8 * per)
            for s in range(8):
                for j in range(cols):
                    for blk, off, done, n in pieces(base + j * per, per, quarter):
                        wg[2 * h + s // 4, s % 4, blk, off : off + n, :] = res[
                            s * per + done : s * per + done + n, j * chans : (j + 1) * chans
                        ]
            base += cols * per
        for blk, off, done, n in pieces(base, PACK - base, quarter):
            wg[2 * h : 2 * h + 2, :, blk, off : off + n, :] = jnp.zeros((2, 4, n, chans), F32)
        for nx in xorder:
            zz = pl.ds(2 * h, 2)
            swaps.append(far.start(wg.at[zz, nx, pl.ds(8 * (1 - rep), 8)], halves.at[zz, nx], other))

    def three(w, u):
        return mm(w[0], u[0], NN) + mm(w[0], u[1], NN) + mm(w[1], u[0], NN)

    firsts = (0, 5 * chans, 13 * chans)

    def keep(order, res):
        rows = res.shape[0]
        rows_ref[firsts[order] : firsts[order] + rows, :] = res[:, :cap]
        if order:
            rows_ref[firsts[order] + rows : firsts[order] + 2 * rows, :] = res[:, cap:]

    def fold(i):
        swaps[i].wait_recv()
        swaps[4 + i].wait_recv()
        nx = xorder[i]
        halves[:, nx] = wg[:, nx, pl.ds(8 * rep, 8)] + halves[:, nx]

    def ring_sum(dst, part, me, copies, ins):
        for copy in copies:
            copy.wait_recv()
        for h in range(2):
            dst(h)[...] = part(me, h)[...] + ins[0, h] + ins[1, h]

    def a_part(nx, h):
        return halves.at[:, nx, pl.ds(2 * h, 2)]

    def b_part(ny, h):
        return halves.at[pl.ds(2 * h, 2), :, 4 + ny]

    def a2_part(ny, h):
        return wa.at[pl.ds(2 * h, 2), ny]

    def b2_part(nx, h):
        return wb.at[pl.ds(2 * h, 2), nx]

    keep(0, three(wh0, u0_ref))
    keep(2, three(wh2r, u2_ref) + three(wh2i, v2_ref))
    fold(0)
    a_first = ring_first(far, x, a_part, a_hops, on_x)
    fold(1)
    fold(2)
    a_rest = ring_own(far, x, a_part, a_ins, on_x)
    fold(3)
    b_first = ring_first(far, y, b_part, b_hops, on_y)
    b_rest = ring_own(far, y, b_part, b_ins, on_y)
    keep(1, three(wh1r, u1_ref) + three(wh1i, v1_ref))
    a_rest += ring_rest(far, x, a_part, a_first, a_hops, a_ins, on_x)
    b_rest += ring_rest(far, y, b_part, b_first, b_hops, b_ins, on_y)

    tiles = cap // 128

    def back(levels, i, carry):
        ch = pl.multiple_of((i // tiles) * 16, 16)
        ln = pl.multiple_of((i % tiles) * 128, 128)
        for level in levels:
            q, cols = min(level, 2), 2 * level + 1
            ds = []
            for r in range(2 * q + 1):
                m = r - q
                k = level - abs(m) + (((5 - abs(m)) if m < 0 else 0))
                ds.append(rows_ref[pl.ds(firsts[abs(m)] + k * chans + ch, 16), pl.ds(ln, 128)])
            for c in range(cols):
                acc = None
                for r in range(2 * q + 1):
                    o = OFFSETS[level] + r * cols + c
                    term = rot_ref[o, :, pl.ds(ln, 128)] * ds[r]
                    acc = term if acc is None else acc + term
                hi, lo = split(acc)
                rows = pl.ds((level * level + c) * chans + ch, 16)
                term_ref[rows, pl.ds(ln, 128)] = hi
                term_ref[rows, pl.ds(ln + cap, 128)] = lo
        return carry

    def f_view(ref, p):
        return ref.at[..., parts[p]]

    def f_part(p):
        return lambda ny, h: total.at[:, ny, pl.ds(8 * h, 8), parts[p]]

    f_first, f_rest = [], []
    for p, (levels, first, width, count) in enumerate(
        ((range(4), 0, 4 * chans, 4), ((4,), 16 * chans, 3 * chans, 3))
    ):
        lax.fori_loop(0, (chans // 16) * tiles, functools.partial(back, levels), 0)

        def scatter(c, carry, first=first, width=width):
            at = pl.multiple_of(first + c * width, 128)
            res = mm(hs2_ref[...], term_ref[pl.ds(at, width), :], NT)
            total[:, :, :, pl.ds(at, width)] = res.reshape(2, 4, 16, width)
            return carry

        lax.fori_loop(0, count, scatter, 0)
        f_first.append(ring_first(far, y, f_part(p), f_view(f_hops, p), on_y))
        f_rest.append(ring_own(far, y, f_part(p), f_view(f_ins, p), on_y))

    def f_on(p):
        f_rest[p] += ring_rest(far, y, f_part(p), f_first[p], f_view(f_hops, p), f_view(f_ins, p), on_y)

    def f_across(p):
        ring_sum(
            lambda h: f_mine.at[:, pl.ds(8 * h, 8), parts[p]], f_part(p), y, f_rest[p], f_view(f_ins, p)
        )
        return far.start(f_mine.at[1 - zh, :, parts[p]], f_got.at[:, parts[p]], across)

    ring_sum(lambda h: wa.at[:, pl.ds(2 * h, 2)], a_part, x, a_rest, a_ins)
    a2_first = ring_first(far, y, a2_part, a2_hops, on_y)
    a2_rest = ring_own(far, y, a2_part, a2_ins, on_y)
    ring_sum(lambda h: wb.at[pl.ds(2 * h, 2)], b_part, y, b_rest, b_ins)
    b2_first = ring_first(far, x, b2_part, b2_hops, on_x)
    b2_rest = ring_own(far, x, b2_part, b2_ins, on_x)
    f_on(0)
    a2_rest += ring_rest(far, y, a2_part, a2_first, a2_hops, a2_ins, on_y)
    b2_rest += ring_rest(far, x, b2_part, b2_first, b2_hops, b2_ins, on_x)
    f_on(1)
    f_swap = [f_across(0)]
    ring_sum(lambda h: w2.at[pl.ds(2 * h, 2), 0], a2_part, y, a2_rest, a2_ins)
    ring_sum(lambda h: w2.at[pl.ds(2 * h, 2), 1], b2_part, x, b2_rest, b2_ins)
    z_made = [far.start(w2.at[a], z_got.at[i], device(rep, a, x, b, y)) for i, (a, b) in enumerate(zs)]
    f_swap.append(f_across(1))
    w3 = w2[zl]
    for i, copy in enumerate(z_made):
        copy.wait_recv()
        w3 = w3 + z_got[i]
    packed[rep, :, y] = w3
    mine = packed.at[rep, :, y]
    ag_made = [far.start(mine, mine, device(a, zl, x, zh, b)) for a, b in ags]
    for copy in f_swap:
        copy.wait_recv()
    out[...] = f_mine[zh] + f_got[...]
    for copy in ag_made:
        copy.wait_recv()
    far.drain()
    line_drain(0)
    line_drain(1)


def finish_kernel(feats, packed, out, o0, o1, o2, o3, o4):
    out[...] = feats[...]
    base = 0
    for o in (o0, o1, o2, o3, o4):
        per = o.shape[0]
        for j in range(o.shape[1] // 128):
            for blk, off, done, n in pieces(base, per, packed.shape[1]):
                o[done : done + n, j * 128 : (j + 1) * 128] = packed[blk, off : off + n, :]
            base += per


def run(src_feats, tgt_cotangent, wig, es, et, cnt, weights, owners, n_tgt):
    cap = es.shape[1]
    chans = 128
    rows, feat = src_feats.shape
    src_blk, tgt_blk = n_tgt * rows, owners * rows
    q = PACK // 16
    vm = pl.BlockSpec(memory_space=pltpu.VMEM)
    anywhere = pl.BlockSpec(memory_space=pl.ANY)
    dims = [w.shape[0] for w in weights]
    count = 2 * 16 + 9 + 8 + 4 * 6 + 2 * 7 + 7 + 7
    feats, packed = pl.pallas_call(
        tile_kernel,
        out_shape=(
            jax.ShapeDtypeStruct((rows, feat), F32),
            jax.ShapeDtypeStruct((2, 2, 4, q, chans), F32),
        ),
        in_specs=[pl.BlockSpec(memory_space=pltpu.SMEM), vm, vm] + [anywhere] * 8,
        out_specs=(vm, vm),
        scratch_shapes=[
            pltpu.VMEM(wig.shape, F32),
            *[pltpu.VMEM((d, d), F32) for d in dims],
            *[pltpu.VMEM((2, d, d), BF16) for d in dims],
            pltpu.VMEM((n_tgt, rows, feat), F32),
            pltpu.VMEM((owners, rows, feat), F32),
            pltpu.VMEM((2 * src_blk, cap), BF16),
            pltpu.VMEM((2 * tgt_blk, cap), BF16),
            pltpu.VMEM((src_blk, 2 * cap), BF16),
            pltpu.VMEM((feat, cap), F32),
            pltpu.VMEM((2, dims[0], cap), BF16),
            pltpu.VMEM((2, dims[1], 2 * cap), BF16),
            pltpu.VMEM((2, dims[3], 2 * cap), BF16),
            pltpu.VMEM((2, dims[0], cap), BF16),
            pltpu.VMEM((2, dims[1], 2 * cap), BF16),
            pltpu.VMEM((2, dims[3], 2 * cap), BF16),
            pltpu.VMEM((2, dims[1], 2 * cap), BF16),
            pltpu.VMEM((2, dims[3], 2 * cap), BF16),
            pltpu.VMEM((feat, 2 * cap), BF16),
            pltpu.VMEM((2, 4, rows, feat), F32),
            pltpu.VMEM((4, 4, 16, q, chans), F32),
            pltpu.VMEM((2, 2, 8, feat), F32),
            pltpu.VMEM((2, 2, 2, 8, feat), F32),
            pltpu.VMEM((2, rows, feat), F32),
            pltpu.VMEM((rows, feat), F32),
            pltpu.VMEM((4, 4, 8, q, chans), F32),
            pltpu.VMEM((2, 4, 2, q, chans), F32),
            pltpu.VMEM((2, 2, 4, 2, q, chans), F32),
            pltpu.VMEM((2, 2, 4, q, chans), F32),
            pltpu.VMEM((2, 2, 2, 4, q, chans), F32),
            pltpu.VMEM((4, 4, q, chans), F32),
            pltpu.VMEM((4, 4, q, chans), F32),
            pltpu.VMEM((2, 2, q, chans), F32),
            pltpu.VMEM((2, 2, 2, q, chans), F32),
            pltpu.VMEM((2, 2, q, chans), F32),
            pltpu.VMEM((2, 2, 2, q, chans), F32),
            pltpu.VMEM((4, 2, q, chans), F32),
            pltpu.VMEM((7, 2, q, chans), F32),
            pltpu.SemaphoreType.DMA((count,)),
            pltpu.SemaphoreType.DMA((count,)),
            pltpu.SemaphoreType.DMA((10,)),
            pltpu.SemaphoreType.DMA((6,)),
            pltpu.SemaphoreType.DMA((8,)),
        ],
        compiler_params=pltpu.CompilerParams(
            collective_id=0, has_side_effects=True, vmem_limit_bytes=62 * 2**20
        ),
        name="tile",
    )(cnt, es, et, src_feats, tgt_cotangent, wig, *weights)
    return pl.pallas_call(
        finish_kernel,
        out_shape=(
            jax.ShapeDtypeStruct((rows, feat), F32),
            *[jax.ShapeDtypeStruct((d // owners, d), F32) for d in dims],
        ),
        in_specs=[vm, vm],
        out_specs=(vm,) * 6,
        name="finish",
    )(feats, packed.reshape(16, q, chans))


def local(src_feats, tgt_cotangent, rotation, edge_src, edge_tgt, edge_count, *weights):
    wig = rotation.transpose(0, 1, 3, 2, 4)[0, 0]
    grad_feats, *grads = run(
        src_feats[0], tgt_cotangent[0], wig, edge_src[0, 0], edge_tgt[0, 0], edge_count[0, 0], weights,
        lax.axis_size("src"), lax.axis_size("tgt"),
    )
    return (grad_feats[None], *grads)


def solution(mesh):
    placed = (
        P("rep", ("src", "tgt"), None),
        P("rep", ("tgt", "src"), None),
        P("rep", "src", "tgt", None, None),
        P("rep", "src", "tgt", None),
        P("rep", "src", "tgt", None),
        P("rep", "src", "tgt"),
        P(), P(), P(), P(), P(),
    )
    return jax.shard_map(
        local,
        mesh=mesh,
        in_specs=placed,
        out_specs=(P("rep", ("src", "tgt"), None), *[P("src", None)] * 5),
        check_vma=False,
    )
```

```python
import functools

import jax
import jax.numpy as jnp
from jax import lax
from jax.experimental import pallas as pl
from jax.experimental.pallas import tpu as pltpu
from jax.sharding import PartitionSpec as P

OFFSETS = (0, 1, 10, 35, 70)
F32, BF16 = jnp.float32, jnp.bfloat16
MESH = pl.DeviceIdType.MESH
PACK = 640
NT = (((1,), (1,)), ((), ()))
NN = (((1,), (0,)), ((), ()))


def mm(a, b, dims):
    return lax.dot_general(a, b, dims, preferred_element_type=F32)


def split(a):
    hi = a.astype(BF16)
    return hi, (a - hi.astype(F32)).astype(BF16)


def onehot(ids, live, atoms):
    rows = lax.broadcasted_iota(jnp.int32, (atoms, ids.shape[1]), 0)
    return jnp.where((rows == ids) & live, 1.0, 0.0).astype(BF16)


def place():
    rep, src, tgt = lax.axis_index("rep"), lax.axis_index("src"), lax.axis_index("tgt")
    return rep, src // 4, src % 4, tgt // 4, tgt % 4


def device(rep, zl, x, zh, y):
    return (rep, zl * 4 + x, zh * 4 + y)


def pair(i, d):
    return (i + 1 - 2 * (i % 2), (i + 2) % 4, 3 - i)[d - 1]


class Copies:
    def __init__(self, send, recv):
        self.send, self.recv, self.made = send, recv, []

    def start(self, src, dst, to):
        n = len(self.made)
        copy = pltpu.make_async_remote_copy(
            src_ref=src, dst_ref=dst, send_sem=self.send.at[n], recv_sem=self.recv.at[n],
            device_id=to, device_id_type=MESH,
        )
        copy.start()
        self.made.append(copy)
        return copy

    def drain(self):
        for copy in self.made:
            copy.wait_send()


def greet(peers):
    barrier = pltpu.get_barrier_semaphore()
    for peer in peers:
        pl.semaphore_signal(barrier, inc=1, device_id=peer, device_id_type=MESH)
    pl.semaphore_wait(barrier, len(peers))


def ring_first(far, me, part, hops, to):
    right, left, opp = (me + 1) % 4, (me + 3) % 4, (me + 2) % 4
    return (
        far.start(part(opp, 0), hops.at[0], to(right)),
        far.start(part(opp, 1), hops.at[1], to(left)),
    )


def ring_own(far, me, part, ins, to):
    right, left = (me + 1) % 4, (me + 3) % 4
    return [
        far.start(part(right, 1), ins.at[0, 1], to(right)),
        far.start(part(left, 0), ins.at[1, 0], to(left)),
    ]


def ring_rest(far, me, part, firsts, hops, ins, to):
    right, left = (me + 1) % 4, (me + 3) % 4
    made = []
    firsts[0].wait_recv()
    hops[0] = hops[0] + part(right, 0)[...]
    made.append(far.start(hops.at[0], ins.at[0, 0], to(right)))
    firsts[1].wait_recv()
    hops[1] = hops[1] + part(left, 1)[...]
    made.append(far.start(hops.at[1], ins.at[1, 1], to(left)))
    return made


def pick(block_ref, hot_ref, out_ref, first, width, count):
    def one(i, carry):
        at = pl.multiple_of(first + i * width, 128)
        block = block_ref[:, :, pl.ds(at, width)]
        hi, lo = split(block.reshape(-1, width).T)
        out_ref[pl.ds(at, width), :] = mm(jnp.concatenate([hi, lo], 1), hot_ref[...], NN)
        return carry

    lax.fori_loop(0, count, one, 0)


def rotate(rows_ref, rot_ref, put, chans, cap, levels):
    steps, lanes = 16, 128
    tiles = cap // lanes

    def one(i, carry):
        ch = pl.multiple_of((i // tiles) * steps, steps)
        ln = pl.multiple_of((i % tiles) * lanes, lanes)
        for level in levels:
            q, cols = min(level, 2), 2 * level + 1
            xs = [
                rows_ref[pl.ds((level * level + c) * chans + ch, steps), pl.ds(ln, lanes)]
                for c in range(cols)
            ]
            for r in range(2 * q + 1):
                acc = None
                for c in range(cols):
                    o = OFFSETS[level] + r * cols + c
                    term = rot_ref[o, :, pl.ds(ln, lanes)] * xs[c]
                    acc = term if acc is None else acc + term
                m = r - q
                put(abs(m), m < 0, level - abs(m), ch, ln, acc)
        return carry

    lax.fori_loop(0, (chans // steps) * tiles, one, 0)


def pieces(first, count, step):
    done = 0
    while done < count:
        blk, off = (first + done) // step, (first + done) % step
        n = min(count - done, step - off)
        yield blk, off, done, n
        done += n


def tile_kernel(
    cnt_ref, es_ref, et_ref, x_in, g_in, rot_in, w0_in, w1r_in, w1i_in, w2r_in, w2i_in,
    out, packed,
    rot_ref, wf0, wf1r, wf1i, wf2r, wf2i, wh0, wh1r, wh1i, wh2r, wh2i,
    x_ref, g_ref, hs_ref, ht_ref, hs2_ref, rows_ref,
    z0_ref, z1_ref, z2_ref, u0_ref, u1_ref, u2_ref, v1_ref, v2_ref, term_ref,
    total, wg, f_hops, f_ins, f_mine, f_got, halves, a_hops, a_ins, b_hops, b_ins,
    wa, wb, a2_hops, a2_ins, b2_hops, b2_ins, w2, z_got,
    send, recv, line_send, line_recv, own,
):
    rep, zl, x, zh, y = place()
    cap, chans, feat = es_ref.shape[1], 128, x_in.shape[1]
    src_blk, tgt_blk = hs_ref.shape[0] // 2, ht_ref.shape[0] // 2
    owned = [
        pltpu.make_async_copy(a, b, own.at[i])
        for i, (a, b) in enumerate(
            ((w0_in, wf0), (w1r_in, wf1r), (w1i_in, wf1i), (w2r_in, wf2r), (w2i_in, wf2i), (rot_in, rot_ref))
        )
    ]

    right, left = (x + 1) % 4, (x + 3) % 4
    up, down = (y + 1) % 4, (y + 3) % 4
    zs = [(pair(zl, d), zh) for d in (1, 2, 3)] + [(zl, 1 - zh)]
    ags = [((rep + dr) % 2, (y + dy) % 4) for dr in (0, 1) for dy in range(4)][1:]
    inner = ((zl + 1) // 2) % 2 == 1
    pair_rest = (pair(zl, 2), pair(zl, 3))
    mate, inward, beyond = pair(zl, 1), 2 - zl // 2, 3 - 3 * (zl // 2)
    across, other = device(rep, zl, x, 1 - zh, y), device(1 - rep, zl, x, zh, y)

    def on_x(nx):
        return device(rep, zl, nx, zh, y)

    def on_y(ny):
        return device(rep, zl, x, zh, ny)

    def on_z(nz):
        return device(rep, nz, x, zh, y)

    greet(
        [on_x(left), on_x(right)]
        + [device(rep, a, x, b, y) for a, b in zs]
        + [device(a, zl, x, zh, b) for a, b in ags]
    )
    far = Copies(send, recv)

    mine_g, mine_x = zl * 4 + x, zh * 4 + y
    parts = (pl.ds(0, 16 * chans), pl.ds(16 * chans, 9 * chans))
    whole = pl.ds(0, feat)

    def both(src, slot, at, out_ref, to, one, two):
        dst = out_ref.at[slot, :, at]
        return far.start(src, dst, to(one)), far.start(src, dst, to(two))

    def relay(copies, out_ref, at, slots, to, one, two):
        copies[0].wait_recv()
        ref = out_ref.at[slots[0], :8, at]
        a = far.start(ref, ref, to(one))
        copies[1].wait_recv()
        ref = out_ref.at[slots[1], 8:, at]
        return a, far.start(ref, ref, to(two))

    xs, ends_g, ends_x, ys = ([], []), ([], []), [], []
    order = [zl, mate, inward, beyond]

    def hand(p, who, sent, got, to):
        dst = g_ref.at[who * 4 + x, :, parts[p]]
        return pltpu.make_async_remote_copy(
            src_ref=g_in.at[:, parts[p]] if who is zl else dst, dst_ref=dst,
            send_sem=line_send.at[5 * p + sent], recv_sem=line_recv.at[3 * p + got],
            device_id=on_z(to), device_id_type=MESH,
        )

    def line_start(p):
        hand(p, zl, 0, 0, mate).start()

        @pl.when(inner)
        def _():
            hand(p, zl, 1, 1, inward).start()

    def line_next(p, k):
        hand(p, order[k + 1], 0, k, mate).wait_recv()

        @pl.when(inner)
        def _():
            if k == 0:
                hand(p, mate, 2, 2, inward).start()
            elif k == 1:
                hand(p, inward, 3, 1, mate).start()
            else:
                hand(p, beyond, 4, 2, mate).start()

    def line_drain(p):
        hand(p, zl, 0, 0, mate).wait_send()

        @pl.when(inner)
        def _():
            for k in range(1, 5):
                hand(p, zl, k, 0, mate).wait_send()

    line_start(0)
    xs[0].append(both(g_in.at[:, parts[0]], mine_g, parts[0], g_ref, on_x, right, left))
    ys.append(both(x_in, mine_x, whole, x_ref, on_y, up, down))
    xs[1].append(both(g_in.at[:, parts[1]], mine_g, parts[1], g_ref, on_x, right, left))
    owned.append(pltpu.make_async_copy(g_in, g_ref.at[mine_g], own.at[6]))
    owned.append(pltpu.make_async_copy(x_in, x_ref.at[mine_x], own.at[7]))
    for copy in owned:
        copy.start()

    def x_step(p, j):
        line_next(p, j - 1)
        slot = order[j] * 4 + x
        xs[p].append(both(g_ref.at[slot, :, parts[p]], slot, parts[p], g_ref, on_x, right, left))

    def x_relay(p, j):
        slots = (order[j] * 4 + left, order[j] * 4 + right)
        ends_g[p].extend(relay(xs[p][j], g_ref, parts[p], slots, on_x, right, left))

    def y_relay(j):
        at = (zh, 1 - zh)[j] * 4
        ends_x.extend(relay(ys[j], x_ref, whole, (at + down, at + up), on_y, up, down))

    live = lax.broadcasted_iota(jnp.int32, (1, cap), 1) < cnt_ref[0]
    hot = onehot(es_ref[...], live, src_blk)
    hs_ref[:src_blk, :] = hot
    hs_ref[src_blk:, :] = hot
    hs2_ref[:, :cap] = hot
    hs2_ref[:, cap:] = hot
    hot = onehot(et_ref[...], live, tgt_blk)
    ht_ref[:tgt_blk, :] = hot
    ht_ref[tgt_blk:, :] = hot
    for copy in owned:
        copy.wait()
    for src, dst in ((wf0, wh0), (wf1r, wh1r), (wf1i, wh1i), (wf2r, wh2r), (wf2i, wh2i)):
        def cut(i, carry, src=src, dst=dst):
            at = pl.ds(pl.multiple_of(i * 128, 128), 128)
            dst[0, at, :], dst[1, at, :] = split(src[at, :])
            return carry

        lax.fori_loop(0, src.shape[0] // 128, cut, 0)

    x_step(0, 1)
    hop = far.start(x_in, x_ref.at[mine_x], across)
    x_relay(0, 0)
    x_step(0, 2)
    line_start(1)
    x_relay(0, 1)
    y_relay(0)
    x_step(0, 3)
    x_relay(0, 2)
    hop.wait_recv()
    slot = (1 - zh) * 4 + y
    ys.append(both(x_ref.at[slot], slot, whole, x_ref, on_y, up, down))
    x_step(1, 1)
    x_relay(0, 3)
    x_relay(1, 0)
    x_step(1, 2)
    y_relay(1)
    x_relay(1, 1)

    zrefs = (z0_ref, z1_ref, z2_ref)

    def put_z(order, neg, k, ch, ln, val):
        hi, lo = split(val)
        rows = pl.ds(k * chans + ch, 16)
        at = pl.ds(ln + (cap if neg else 0), 128)
        zrefs[order][0, rows, at] = hi
        zrefs[order][1, rows, at] = lo

    x_step(1, 3)
    for copy in ends_x:
        copy.wait_recv()
    pick(x_ref, hs_ref, rows_ref, 0, 5 * chans, 5)
    x_relay(1, 2)
    x_relay(1, 3)
    rotate(rows_ref, rot_ref, put_z, chans, cap, range(5))

    urefs = (u0_ref, u1_ref, u2_ref)
    vrefs = (None, v1_ref, v2_ref)

    def put_u(order, neg, k, ch, ln, val):
        hi, lo = split(val)
        rows = pl.ds(k * chans + ch, 16)
        at = pl.ds(ln + (cap if neg else 0), 128)
        urefs[order][0, rows, at] = hi
        urefs[order][1, rows, at] = lo
        if order:
            at = pl.ds(ln + (0 if neg else cap), 128)
            vrefs[order][0, rows, at] = hi if neg else -hi
            vrefs[order][1, rows, at] = lo if neg else -lo

    for copy in ends_g[0]:
        copy.wait_recv()
    pick(g_ref, ht_ref, rows_ref, 0, 4 * chans, 4)
    rotate(rows_ref, rot_ref, put_u, chans, cap, range(4))
    for copy in ends_g[1]:
        copy.wait_recv()
    pick(g_ref, ht_ref, rows_ref, 16 * chans, 3 * chans, 3)
    rotate(rows_ref, rot_ref, put_u, chans, cap, (4,))

    def grad(z, u, at, count):
        zhi, zlo = z[0, pl.ds(at, count), :], z[1, pl.ds(at, count), :]
        return mm(jnp.concatenate([zhi, zhi, zlo], 1), jnp.concatenate([u[0], u[1], u[0]], 1), NT)

    quarter = wg.shape[3]
    xorder = [(x + 2) % 4, right, left, x]
    swaps = []
    for h in range(2):
        base = 0
        for zr, ur, cols in (
            (z0_ref, u0_ref, 5), (z1_ref, u1_ref, 4), (z1_ref, v1_ref, 4), (z2_ref, u2_ref, 3), (z2_ref, v2_ref, 3),
        ):
            per = cols * chans // 16
            res = grad(zr, ur, h * 8 * per, 8 * per)
            for s in range(8):
                for j in range(cols):
                    for blk, off, done, n in pieces(base + j * per, per, quarter):
                        wg[2 * h + s // 4, s % 4, blk, off : off + n, :] = res[
                            s * per + done : s * per + done + n, j * chans : (j + 1) * chans
                        ]
            base += cols * per
        for blk, off, done, n in pieces(base, PACK - base, quarter):
            wg[2 * h : 2 * h + 2, :, blk, off : off + n, :] = jnp.zeros((2, 4, n, chans), F32)
        for nx in xorder:
            zz = pl.ds(2 * h, 2)
            swaps.append(far.start(wg.at[zz, nx, pl.ds(8 * (1 - rep), 8)], halves.at[zz, nx], other))

    def three(w, u):
        return mm(jnp.concatenate([w[0], w[0], w[1]], 1), jnp.concatenate([u[0], u[1], u[0]], 0), NN)

    firsts = (0, 5 * chans, 13 * chans)

    def keep(order, res):
        rows = res.shape[0]
        rows_ref[firsts[order] : firsts[order] + rows, :] = res[:, :cap]
        if order:
            rows_ref[firsts[order] + rows : firsts[order] + 2 * rows, :] = res[:, cap:]

    def fold(i):
        swaps[i].wait_recv()
        swaps[4 + i].wait_recv()
        nx = xorder[i]
        halves[:, nx] = wg[:, nx, pl.ds(8 * rep, 8)] + halves[:, nx]

    def ring_sum(dst, part, me, copies, ins):
        for copy in copies:
            copy.wait_recv()
        for h in range(2):
            dst(h)[...] = part(me, h)[...] + ins[0, h] + ins[1, h]

    def a_part(nx, h):
        return halves.at[:, nx, pl.ds(2 * h, 2)]

    def b_part(ny, h):
        return halves.at[pl.ds(2 * h, 2), :, 4 + ny]

    def a2_part(ny, h):
        return wa.at[pl.ds(2 * h, 2), ny]

    def b2_part(nx, h):
        return wb.at[pl.ds(2 * h, 2), nx]

    keep(0, three(wh0, u0_ref))
    keep(2, three(wh2r, u2_ref) + three(wh2i, v2_ref))
    fold(0)
    a_first = ring_first(far, x, a_part, a_hops, on_x)
    fold(1)
    fold(2)
    a_rest = ring_own(far, x, a_part, a_ins, on_x)
    fold(3)
    b_first = ring_first(far, y, b_part, b_hops, on_y)
    b_rest = ring_own(far, y, b_part, b_ins, on_y)
    keep(1, three(wh1r, u1_ref) + three(wh1i, v1_ref))
    a_rest += ring_rest(far, x, a_part, a_first, a_hops, a_ins, on_x)
    b_rest += ring_rest(far, y, b_part, b_first, b_hops, b_ins, on_y)

    tiles = cap // 128

    def back(levels, i, carry):
        ch = pl.multiple_of((i // tiles) * 16, 16)
        ln = pl.multiple_of((i % tiles) * 128, 128)
        for level in levels:
            q, cols = min(level, 2), 2 * level + 1
            ds = []
            for r in range(2 * q + 1):
                m = r - q
                k = level - abs(m) + (((5 - abs(m)) if m < 0 else 0))
                ds.append(rows_ref[pl.ds(firsts[abs(m)] + k * chans + ch, 16), pl.ds(ln, 128)])
            for c in range(cols):
                acc = None
                for r in range(2 * q + 1):
                    o = OFFSETS[level] + r * cols + c
                    term = rot_ref[o, :, pl.ds(ln, 128)] * ds[r]
                    acc = term if acc is None else acc + term
                hi, lo = split(acc)
                rows = pl.ds((level * level + c) * chans + ch, 16)
                term_ref[rows, pl.ds(ln, 128)] = hi
                term_ref[rows, pl.ds(ln + cap, 128)] = lo
        return carry

    def f_view(ref, p):
        return ref.at[..., parts[p]]

    def f_part(p):
        return lambda ny, h: total.at[:, ny, pl.ds(8 * h, 8), parts[p]]

    f_first, f_rest = [], []
    for p, (levels, first, width, count) in enumerate(
        ((range(4), 0, 4 * chans, 4), ((4,), 16 * chans, 3 * chans, 3))
    ):
        lax.fori_loop(0, (chans // 16) * tiles, functools.partial(back, levels), 0)

        def scatter(c, carry, first=first, width=width):
            at = pl.multiple_of(first + c * width, 128)
            res = mm(term_ref[pl.ds(at, width), :], hs2_ref[...], NT).T
            total[:, :, :, pl.ds(at, width)] = res.reshape(2, 4, 16, width)
            return carry

        lax.fori_loop(0, count, scatter, 0)
        f_first.append(ring_first(far, y, f_part(p), f_view(f_hops, p), on_y))
        f_rest.append(ring_own(far, y, f_part(p), f_view(f_ins, p), on_y))

    def f_on(p):
        f_rest[p] += ring_rest(far, y, f_part(p), f_first[p], f_view(f_hops, p), f_view(f_ins, p), on_y)

    def f_across(p):
        ring_sum(
            lambda h: f_mine.at[:, pl.ds(8 * h, 8), parts[p]], f_part(p), y, f_rest[p], f_view(f_ins, p)
        )
        return far.start(f_mine.at[1 - zh, :, parts[p]], f_got.at[:, parts[p]], across)

    ring_sum(lambda h: wa.at[:, pl.ds(2 * h, 2)], a_part, x, a_rest, a_ins)
    a2_first = ring_first(far, y, a2_part, a2_hops, on_y)
    a2_rest = ring_own(far, y, a2_part, a2_ins, on_y)
    ring_sum(lambda h: wb.at[pl.ds(2 * h, 2)], b_part, y, b_rest, b_ins)
    b2_first = ring_first(far, x, b2_part, b2_hops, on_x)
    b2_rest = ring_own(far, x, b2_part, b2_ins, on_x)
    f_on(0)
    a2_rest += ring_rest(far, y, a2_part, a2_first, a2_hops, a2_ins, on_y)
    b2_rest += ring_rest(far, x, b2_part, b2_first, b2_hops, b2_ins, on_x)
    f_on(1)
    f_swap = [f_across(0)]
    ring_sum(lambda h: w2.at[pl.ds(2 * h, 2), 0], a2_part, y, a2_rest, a2_ins)
    ring_sum(lambda h: w2.at[pl.ds(2 * h, 2), 1], b2_part, x, b2_rest, b2_ins)
    z_made = [far.start(w2.at[a], z_got.at[i], on_z(a)) for i, a in enumerate((mate, *pair_rest))]
    f_swap.append(f_across(1))
    w3 = w2[zl]
    for i, copy in enumerate(z_made):
        copy.wait_recv()
        w3 = w3 + z_got[i]
    z_got[3] = w3
    swap = far.start(z_got.at[3], z_got.at[4], across)
    swap.wait_recv()
    w3 = w3 + z_got[4]
    packed[rep, :, y] = w3
    mine = packed.at[rep, :, y]
    ag_made = [far.start(mine, mine, device(a, zl, x, zh, b)) for a, b in ags]
    for copy in f_swap:
        copy.wait_recv()
    out[...] = f_mine[zh] + f_got[...]
    for copy in ag_made:
        copy.wait_recv()
    far.drain()
    line_drain(0)
    line_drain(1)


def finish_kernel(feats, packed, out, o0, o1, o2, o3, o4):
    out[...] = feats[...]
    base = 0
    for o in (o0, o1, o2, o3, o4):
        per = o.shape[0]
        for j in range(o.shape[1] // 128):
            for blk, off, done, n in pieces(base, per, packed.shape[1]):
                o[done : done + n, j * 128 : (j + 1) * 128] = packed[blk, off : off + n, :]
            base += per


def run(src_feats, tgt_cotangent, wig, es, et, cnt, weights, owners, n_tgt):
    cap = es.shape[1]
    chans = 128
    rows, feat = src_feats.shape
    src_blk, tgt_blk = n_tgt * rows, owners * rows
    q = PACK // 16
    vm = pl.BlockSpec(memory_space=pltpu.VMEM)
    anywhere = pl.BlockSpec(memory_space=pl.ANY)
    dims = [w.shape[0] for w in weights]
    count = 2 * 16 + 9 + 8 + 4 * 6 + 2 * 7 + 7 + 7
    feats, packed = pl.pallas_call(
        tile_kernel,
        out_shape=(
            jax.ShapeDtypeStruct((rows, feat), F32),
            jax.ShapeDtypeStruct((2, 2, 4, q, chans), F32),
        ),
        in_specs=[pl.BlockSpec(memory_space=pltpu.SMEM), vm, vm] + [anywhere] * 8,
        out_specs=(vm, vm),
        scratch_shapes=[
            pltpu.VMEM(wig.shape, F32),
            *[pltpu.VMEM((d, d), F32) for d in dims],
            *[pltpu.VMEM((2, d, d), BF16) for d in dims],
            pltpu.VMEM((n_tgt, rows, feat), F32),
            pltpu.VMEM((owners, rows, feat), F32),
            pltpu.VMEM((2 * src_blk, cap), BF16),
            pltpu.VMEM((2 * tgt_blk, cap), BF16),
            pltpu.VMEM((src_blk, 2 * cap), BF16),
            pltpu.VMEM((feat, cap), F32),
            pltpu.VMEM((2, dims[0], cap), BF16),
            pltpu.VMEM((2, dims[1], 2 * cap), BF16),
            pltpu.VMEM((2, dims[3], 2 * cap), BF16),
            pltpu.VMEM((2, dims[0], cap), BF16),
            pltpu.VMEM((2, dims[1], 2 * cap), BF16),
            pltpu.VMEM((2, dims[3], 2 * cap), BF16),
            pltpu.VMEM((2, dims[1], 2 * cap), BF16),
            pltpu.VMEM((2, dims[3], 2 * cap), BF16),
            pltpu.VMEM((feat, 2 * cap), BF16),
            pltpu.VMEM((2, 4, rows, feat), F32),
            pltpu.VMEM((4, 4, 16, q, chans), F32),
            pltpu.VMEM((2, 2, 8, feat), F32),
            pltpu.VMEM((2, 2, 2, 8, feat), F32),
            pltpu.VMEM((2, rows, feat), F32),
            pltpu.VMEM((rows, feat), F32),
            pltpu.VMEM((4, 4, 8, q, chans), F32),
            pltpu.VMEM((2, 4, 2, q, chans), F32),
            pltpu.VMEM((2, 2, 4, 2, q, chans), F32),
            pltpu.VMEM((2, 2, 4, q, chans), F32),
            pltpu.VMEM((2, 2, 2, 4, q, chans), F32),
            pltpu.VMEM((4, 4, q, chans), F32),
            pltpu.VMEM((4, 4, q, chans), F32),
            pltpu.VMEM((2, 2, q, chans), F32),
            pltpu.VMEM((2, 2, 2, q, chans), F32),
            pltpu.VMEM((2, 2, q, chans), F32),
            pltpu.VMEM((2, 2, 2, q, chans), F32),
            pltpu.VMEM((4, 2, q, chans), F32),
            pltpu.VMEM((5, 2, q, chans), F32),
            pltpu.SemaphoreType.DMA((count,)),
            pltpu.SemaphoreType.DMA((count,)),
            pltpu.SemaphoreType.DMA((10,)),
            pltpu.SemaphoreType.DMA((6,)),
            pltpu.SemaphoreType.DMA((8,)),
        ],
        compiler_params=pltpu.CompilerParams(
            collective_id=0, has_side_effects=True, vmem_limit_bytes=62 * 2**20
        ),
        name="tile",
    )(cnt, es, et, src_feats, tgt_cotangent, wig, *weights)
    return pl.pallas_call(
        finish_kernel,
        out_shape=(
            jax.ShapeDtypeStruct((rows, feat), F32),
            *[jax.ShapeDtypeStruct((d // owners, d), F32) for d in dims],
        ),
        in_specs=[vm, vm],
        out_specs=(vm,) * 6,
        name="finish",
    )(feats, packed.reshape(16, q, chans))


def local(src_feats, tgt_cotangent, rotation, edge_src, edge_tgt, edge_count, *weights):
    wig = rotation.transpose(0, 1, 3, 2, 4)[0, 0]
    grad_feats, *grads = run(
        src_feats[0], tgt_cotangent[0], wig, edge_src[0, 0], edge_tgt[0, 0], edge_count[0, 0], weights,
        lax.axis_size("src"), lax.axis_size("tgt"),
    )
    return (grad_feats[None], *grads)


def solution(mesh):
    placed = (
        P("rep", ("src", "tgt"), None),
        P("rep", ("tgt", "src"), None),
        P("rep", "src", "tgt", None, None),
        P("rep", "src", "tgt", None),
        P("rep", "src", "tgt", None),
        P("rep", "src", "tgt"),
        P(), P(), P(), P(), P(),
    )
    return jax.shard_map(
        local,
        mesh=mesh,
        in_specs=placed,
        out_specs=(P("rep", ("src", "tgt"), None), *[P("src", None)] * 5),
        check_vma=False,
    )
```
